256 devices in a mesh: chan: 32 (over x_hi, z, core), win: 8 (over y, x_lo).
Axes of the slice: x: 4 (x_hi: 2, x_lo: 2; x = x_hi * 2 + x_lo), y: 4, z: 8, core: 2. Of those that a mesh axis runs over, the one named last changes fastest.
Arguments:
- spectra: bfloat16 [2, 16, 4096, 4096], P(None, 'win', 'chan'), may hold values from -6 to 6
- exponents: int32 [16, 4096, 32], P('win', 'chan'), may hold values from -1 to 1
- source_channels: int32 [1], replicated, may hold values from 0 to 4095
Outputs:
- correlations: float32 [1, 4096, 2048], P(None, 'chan', 'win')
The draws below stay inside these ranges and needn't reach their ends.
All inputs are finite; a program needn't handle non-finite values.
Results may differ from the reference program's by a relative error of at most 0.0003.
Values sent between devices are 32-bit elements; how exact they have to be, the bound alone decides.
No kernel may reach another device: no remote copies, remote signals or barrier semaphores. Data moves between devices by JAX's collectives and lax.ppermute only.
A program may use at most 64 MiB of HBM per device.

```python
import math
import jax
import jax.numpy as jnp
from jax import lax

F = 4096
L = 2048
BLK = 128
S = 1
C = 4096
NSEG = 16


def touch_ends(array, rng, least, top_value):
    dims = array.shape
    place = [jax.random.randint(jax.random.fold_in(rng, axis), (), 0, dims[axis]) for axis in range(len(dims))]
    array = array.at[tuple(place)].set(least)
    longest = dims.index(max(dims))
    place[longest] = (place[longest] + 1) % dims[longest]
    return array.at[tuple(place)].set(top_value)


def block_scale(stream_key, shape, cuts, low, top_value):
    def one(position, blocks):
        heights = jax.random.uniform(jax.random.fold_in(jax.random.fold_in(stream_key, 6), position), (blocks,), jnp.float32, low / len(cuts), top_value / len(cuts))
        return jnp.repeat(jnp.exp(heights), shape[position] // blocks).reshape((-1,) + (1,) * (len(shape) - position - 1))

    loudness = one(*cuts[0])
    for cut in cuts[1:]:
        loudness = loudness * one(*cut)
    return loudness


def gaussian(rng, dims, scale, most, cuts=(), dtype=jnp.bfloat16):
    drawn = scale * jax.random.normal(rng, dims, jnp.float32)
    if cuts:
        drawn = drawn * block_scale(rng, dims, cuts, -0.22, 0.18)
    return jnp.clip(drawn, -most, most).astype(dtype)


def setup_inputs(seed: int = 0) -> dict:
    keys = jax.random.split(jax.random.key(seed), 4)
    spectra = gaussian(keys[0], (2, NSEG, C, F), 1.0, 6.0, ((1, 8), (2, 32)))
    exponents = touch_ends(jax.random.randint(keys[1], (NSEG, C, F // BLK), -1, 2), jax.random.fold_in(keys[1], 1), -1, 1).astype(jnp.int32)
    source_channels = jax.random.randint(keys[2], (S,), 0, C).astype(jnp.int32)
    return dict(spectra=spectra, exponents=exponents, source_channels=source_channels)


def dequantize(spectra, exponents):
    scale = jnp.exp2(exponents.astype(jnp.float32))
    scale = jnp.repeat(scale, BLK, axis=2)
    return spectra.astype(jnp.float32) * scale[None]

def reference(spectra, exponents, source_channels):
    values = dequantize(spectra, exponents)
    slab = jnp.take(values, source_channels.astype(jnp.int32), axis=2)
    high = lax.Precision.HIGHEST
    real_part = jnp.einsum('gsf,gcf->scf', slab[0], values[0], precision=high) + jnp.einsum('gsf,gcf->scf', slab[1], values[1], precision=high)
    imag_part = jnp.einsum('gsf,gcf->scf', slab[0], values[1], precision=high) - jnp.einsum('gsf,gcf->scf', slab[1], values[0], precision=high)
    padded_real = jnp.concatenate([real_part, jnp.zeros_like(real_part)], axis=2)
    padded_imag = jnp.concatenate([imag_part, jnp.zeros_like(imag_part)], axis=2)
    spectrum = padded_real + 1j * padded_imag
    period = 2 * F
    inverse = jnp.real(jnp.fft.ifft(spectrum, axis=2)) * period
    lagged = jnp.concatenate([inverse[:, :, period - L // 2:], inverse[:, :, :L // 2]], axis=2)
    norm = 1.0 / math.sqrt(4.0 * F * NSEG)
    return lagged * norm
```

```python
import math

import jax
import jax.numpy as jnp
import numpy as np
from jax import lax
from jax.experimental import pallas as pl
from jax.experimental.pallas import tpu as pltpu
from jax.sharding import PartitionSpec as P

F = 4096
L = 2048
RES = 8
SPAN = 2 * F // RES
COLS = L // RES
LANES = 128
ROWS = 16
ROOT = math.sqrt(0.5)


def tables(norm):
    bins = np.arange(SPAN)
    lag = np.arange(COLS) - COLS // 2
    angle = 2.0 * np.pi * ((bins[:, None] * lag[None, :]) % SPAN) / SPAN
    parts = np.stack([np.cos(angle), -np.sin(angle)], 0) * norm
    parts = parts.reshape(2, SPAN // LANES, LANES, COLS).transpose(1, 0, 2, 3)
    whole = parts.reshape(2 * SPAN, COLS)
    high = whole.astype(jnp.bfloat16)
    low = (whole - high.astype(np.float64)).astype(jnp.bfloat16)
    turn = 2.0 * np.pi * (np.arange(RES)[:, None] * bins[None, :]) / (2 * F)
    twiddle = np.stack([np.cos(turn), np.sin(turn)], 1).reshape(2 * RES, SPAN)
    return high, low, twiddle.astype(np.float32)


def dequantize_kernel(codes_ref, exponents_ref, values_ref):
    scale = jnp.exp2(exponents_ref[0].astype(jnp.float32)).T
    for block in range(scale.shape[1]):
        wide = jnp.broadcast_to(scale[:, block : block + 1], (scale.shape[0], LANES))
        wide = wide.astype(jnp.bfloat16)
        at = pl.ds(block * LANES, LANES)
        for part in range(2):
            values_ref[part, 0, :, at] = codes_ref[part, 0, :, at] * wide


def dequantize(spectra, exponents):
    _, segs, chans, nbin = spectra.shape
    lanes = jnp.transpose(exponents, (0, 2, 1))
    return pl.pallas_call(
        dequantize_kernel,
        grid=(segs,),
        in_specs=[
            pl.BlockSpec((2, 1, chans, nbin), lambda g: (0, g, 0, 0)),
            pl.BlockSpec((1, lanes.shape[1], chans), lambda g: (g, 0, 0)),
        ],
        out_specs=pl.BlockSpec((2, 1, chans, nbin), lambda g: (0, g, 0, 0)),
        out_shape=jax.ShapeDtypeStruct(spectra.shape, jnp.bfloat16),
        compiler_params=pltpu.CompilerParams(vmem_limit_bytes=20 << 20),
        name="dequantize",
    )(spectra, lanes)


def times_root(re, im):
    return (re - im) * ROOT, (re + im) * ROOT


def four(x):
    (ar, ai), (br, bi), (cr, ci), (dr, di) = x
    sr, si, tr, ti = ar + cr, ai + ci, ar - cr, ai - ci
    ur, ui, vr, vi = br + dr, bi + di, br - dr, bi - di
    return [(sr + ur, si + ui), (tr - vi, ti + vr), (sr - ur, si - ui), (tr + vi, ti - vr)]


def lags_kernel(base, values_ref, slab_ref, twiddle_ref, high_ref, low_ref, out_ref, hi_ref, lo_ref, acc_ref):
    chans = out_ref.shape[1]
    segs = values_ref.shape[1]
    steps = SPAN // LANES

    def produce(n, slot):
        def at(j):
            return pl.ds(pl.multiple_of(j * SPAN + n * LANES, LANES), LANES)

        for r in range(0, chans, ROWS):
            x = []
            for j in range(RES // 2):
                re = im = None
                for g in range(segs):
                    vr = values_ref[0, g, pl.ds(base + r, ROWS), at(j)].astype(jnp.float32)
                    vi = values_ref[1, g, pl.ds(base + r, ROWS), at(j)].astype(jnp.float32)
                    sr = slab_ref[pl.ds(g, 1), at(j)]
                    si = slab_ref[pl.ds(segs + g, 1), at(j)]
                    pr = sr * vr + si * vi
                    pi = sr * vi - si * vr
                    re = pr if re is None else re + pr
                    im = pi if im is None else im + pi
                x.append((re, im))
            even = four(x)
            (br, bi), (dr, di) = x[1], x[3]
            odd = four(
                [
                    x[0],
                    times_root(br, bi),
                    (-x[2][1], x[2][0]),
                    ((-dr - di) * ROOT, (dr - di) * ROOT),
                ]
            )
            for u in range(RES):
                gr, gi = even[u // 2] if u % 2 == 0 else odd[u // 2]
                if u:
                    cos = twiddle_ref[pl.ds(2 * u, 1), at(0)]
                    sin = twiddle_ref[pl.ds(2 * u + 1, 1), at(0)]
                    gr, gi = gr * cos - gi * sin, gr * sin + gi * cos
                for k, part in enumerate((gr, gi)):
                    top = part.astype(jnp.bfloat16)
                    rest = (part - top.astype(jnp.float32)).astype(jnp.bfloat16)
                    where = (slot, pl.ds(u * chans + r, ROWS), pl.ds(k * LANES, LANES))
                    hi_ref[where] = top
                    lo_ref[where] = rest

    def contract(n, slot):
        rows = pl.ds(pl.multiple_of(n * 2 * LANES, 2 * LANES), 2 * LANES)
        whi = high_ref[rows, :]
        hi = hi_ref[slot]
        dot = lambda a, b: jnp.dot(a, b, preferred_element_type=jnp.float32)
        return dot(hi, whi) + dot(lo_ref[slot], whi) + dot(hi, low_ref[rows, :])

    produce(0, 0)
    acc_ref[...] = jnp.zeros_like(acc_ref)

    def step(n, carry):
        produce(n, n % 2)
        acc_ref[...] += contract(n - 1, (n - 1) % 2)
        return carry

    lax.fori_loop(1, steps, step, 0)
    acc_ref[...] += contract(steps - 1, (steps - 1) % 2)

    piece = COLS // RES
    per = LANES // piece
    lane = lax.broadcasted_iota(jnp.int32, (8, LANES), 1)
    for r in range(0, chans, 8):
        turned = []
        for u in range(RES):
            halves = [acc_ref[pl.ds(u * chans + r, 8), pl.ds(h * LANES, LANES)] for h in range(2)]
            shift = piece * u
            if shift >= LANES:
                halves = halves[::-1]
                shift -= LANES
            if shift:
                a, b = (pltpu.roll(x, shift, 1) for x in halves)
                head = lane < shift
                halves = [jnp.where(head, b, a), jnp.where(head, a, b)]
            turned.append(halves)
        for w in range(RES):
            for h in range(2):
                picks = [turned[(h * per + s - w) % RES][h] for s in range(per)]
                left = jnp.where(lane < piece, picks[0], picks[1])
                right = jnp.where(lane < 3 * piece, picks[2], picks[3])
                out_ref[w, pl.ds(r, 8), pl.ds(h * LANES, LANES)] = jnp.where(lane < 2 * piece, left, right)


def partial_lags(values, slab, tabs, base, chans):
    high, low, twiddle = tabs
    vmem = pl.BlockSpec(memory_space=pltpu.VMEM)
    return pl.pallas_call(
        lambda *refs: lags_kernel(base, *refs),
        in_specs=[vmem] * 5,
        out_specs=vmem,
        out_shape=jax.ShapeDtypeStruct((RES, chans, COLS), jnp.float32),
        scratch_shapes=[
            pltpu.VMEM((2, RES * chans, 2 * LANES), jnp.bfloat16),
            pltpu.VMEM((2, RES * chans, 2 * LANES), jnp.bfloat16),
            pltpu.VMEM((RES * chans, COLS), jnp.float32),
        ],
        compiler_params=pltpu.CompilerParams(vmem_limit_bytes=16 << 20),
        name="lags",
    )(values, slab, twiddle, high, low)


def finish_kernel(own_ref, tiles_ref, out_ref):
    total = tiles_ref[0]
    for peer in range(1, tiles_ref.shape[0]):
        total = total + tiles_ref[peer]
    piece = COLS // RES
    place = lax.broadcasted_iota(jnp.int32, (COLS, COLS), 0)
    lag = lax.broadcasted_iota(jnp.int32, (COLS, COLS), 1)
    residue = (place // piece - own_ref[0] + RES) % RES
    order = jnp.where(lag == place % piece * RES + residue, 1.0, 0.0).astype(jnp.bfloat16)
    first = total.astype(jnp.bfloat16)
    rest = total - first.astype(jnp.float32)
    second = rest.astype(jnp.bfloat16)
    third = (rest - second.astype(jnp.float32)).astype(jnp.bfloat16)
    dot = lambda a: jnp.dot(a, order, preferred_element_type=jnp.float32)
    out_ref[...] = (dot(third) + dot(second)) + dot(first)


def finish(own, tiles):
    return pl.pallas_call(
        finish_kernel,
        in_specs=[pl.BlockSpec(memory_space=pltpu.SMEM), pl.BlockSpec(memory_space=pltpu.VMEM)],
        out_specs=pl.BlockSpec(memory_space=pltpu.VMEM),
        out_shape=jax.ShapeDtypeStruct(tiles.shape[1:], jnp.float32),
        compiler_params=pltpu.CompilerParams(vmem_limit_bytes=8 << 20),
        name="finish",
    )(own, tiles)


def own_slab(spectra, exponents, source_channels):
    local_count = spectra.shape[2]
    local_index = source_channels[0] - lax.axis_index("chan") * local_count
    owned = (local_index >= 0) & (local_index < local_count)
    clipped = jnp.clip(local_index, 0, local_count - 1)
    codes = lax.dynamic_index_in_dim(spectra, clipped, 2, keepdims=False).astype(jnp.float32)
    scale = jnp.exp2(lax.dynamic_index_in_dim(exponents, clipped, 1, keepdims=False).astype(jnp.float32))
    scale = jnp.where(owned, scale, 0.0)
    block = spectra.shape[3] // exponents.shape[2]
    return codes * jnp.repeat(scale, block, axis=1)[None]


def spread(slab):
    peers = lax.axis_size("chan")
    tiles = lax.all_to_all(slab.reshape(peers, -1), "chan", 0, 0, tiled=True)
    own = jnp.sum(tiles, axis=0)
    whole = lax.all_to_all(jnp.broadcast_to(own[None], (peers, own.shape[0])), "chan", 0, 0, tiled=True)
    return whole.reshape(4, -1)


def body(spectra, exponents, source_channels):
    chans = spectra.shape[2]
    segs = spectra.shape[1] * lax.axis_size("win")
    slab = spread(own_slab(spectra, exponents, source_channels))
    values = dequantize(spectra, exponents)
    tabs = tables(1.0 / math.sqrt(4.0 * F * segs))
    partial = partial_lags(values, slab, tabs, 0, chans)
    tiles = lax.all_to_all(partial, "win", 0, 0, tiled=True)
    own = lax.axis_index("win").reshape(1).astype(jnp.int32)
    return finish(own, tiles)[None]


def solution(mesh):
    return jax.shard_map(
        body,
        mesh=mesh,
        in_specs=(P(None, "win", "chan", None), P("win", "chan", None), P()),
        out_specs=P(None, "chan", "win"),
        check_vma=False,
    )
```

```python
import math

import jax
import jax.numpy as jnp
import numpy as np
from jax import lax
from jax.experimental import pallas as pl
from jax.experimental.pallas import tpu as pltpu
from jax.sharding import PartitionSpec as P

F = 4096
L = 2048
RES = 8
SPAN = 2 * F // RES
COLS = L // RES
LANES = 128
ROWS = 16
ROOT = math.sqrt(0.5)


def tables(norm):
    bins = np.arange(SPAN)
    lag = np.arange(COLS) - COLS // 2
    angle = 2.0 * np.pi * ((bins[:, None] * lag[None, :]) % SPAN) / SPAN
    parts = np.stack([np.cos(angle), -np.sin(angle)], 0) * norm
    parts = parts.reshape(2, SPAN // LANES, LANES, COLS).transpose(1, 0, 2, 3)
    whole = parts.reshape(2 * SPAN, COLS)
    high = whole.astype(jnp.bfloat16)
    low = (whole - high.astype(np.float64)).astype(jnp.bfloat16)
    turn = 2.0 * np.pi * (np.arange(RES)[:, None] * bins[None, :]) / (2 * F)
    twiddle = np.stack([np.cos(turn), np.sin(turn)], 1).reshape(2 * RES, SPAN)
    return high, low, twiddle.astype(np.float32)


def dequantize_kernel(codes_ref, exponents_ref, values_ref):
    seg = pl.program_id(0)
    scale = jnp.exp2(exponents_ref[0].astype(jnp.float32)).T
    for block in range(scale.shape[1]):
        wide = jnp.broadcast_to(scale[:, block : block + 1], (scale.shape[0], LANES))
        wide = wide.astype(jnp.bfloat16)
        at = pl.ds(block * LANES, LANES)
        for part in range(2):
            values_ref[part, seg, :, at] = codes_ref[part, 0, :, at] * wide


def dequantize(spectra, lanes):
    _, segs, chans, nbin = spectra.shape
    return pl.pallas_call(
        dequantize_kernel,
        grid=(segs,),
        in_specs=[
            pl.BlockSpec((2, 1, chans, nbin), lambda g: (0, g, 0, 0)),
            pl.BlockSpec((1, lanes.shape[1], chans), lambda g: (g, 0, 0)),
        ],
        out_specs=pl.BlockSpec(memory_space=pltpu.VMEM),
        out_shape=jax.ShapeDtypeStruct(spectra.shape, jnp.bfloat16),
        compiler_params=pltpu.CompilerParams(vmem_limit_bytes=20 << 20),
        name="dequantize",
    )(spectra, lanes)


def pick_kernel(local_ref, codes_ref, exponents_ref, slab_ref, rows_ref, lanes_ref, row_sem, lane_sem):
    segs, blocks, chans = lanes_ref.shape
    local = local_ref[0]
    owned = (local >= 0) & (local < chans)
    row = jnp.clip(local, 0, chans - 1)
    first = pl.multiple_of(row // ROWS * ROWS, ROWS)
    rows_in = pltpu.make_async_copy(codes_ref.at[:, :, pl.ds(first, ROWS), :], rows_ref, row_sem)
    lanes_in = pltpu.make_async_copy(exponents_ref, lanes_ref, lane_sem)
    rows_in.start()
    lanes_in.start()
    own_lane = lax.broadcasted_iota(jnp.int32, (blocks, chans), 1) == row
    own_row = lax.broadcasted_iota(jnp.int32, (ROWS, LANES), 0) == row % ROWS
    lanes_in.wait()
    rows_in.wait()
    for g in range(segs):
        exponent = jnp.sum(jnp.where(own_lane, lanes_ref[g].astype(jnp.float32), 0.0), axis=1, keepdims=True)
        scale = jnp.where(owned, jnp.exp2(exponent), 0.0)
        scale = jnp.broadcast_to(scale, (blocks, LANES)).astype(jnp.bfloat16).astype(jnp.float32)
        for part in range(2):
            for block in range(blocks):
                at = pl.ds(block * LANES, LANES)
                codes = rows_ref[part, g, :, at].astype(jnp.float32)
                code = jnp.sum(jnp.where(own_row, codes, 0.0), axis=0, keepdims=True)
                slab_ref[pl.ds(part * segs + g, 1), at] = code * scale[block : block + 1]


def pick(local, spectra, lanes):
    _, segs, _, nbin = spectra.shape
    hbm = pl.BlockSpec(memory_space=pltpu.MemorySpace.HBM)
    return pl.pallas_call(
        pick_kernel,
        in_specs=[pl.BlockSpec(memory_space=pltpu.SMEM), hbm, hbm],
        out_specs=pl.BlockSpec(memory_space=pltpu.VMEM),
        out_shape=jax.ShapeDtypeStruct((2 * segs, nbin), jnp.float32),
        scratch_shapes=[
            pltpu.VMEM((2, segs, ROWS, nbin), jnp.bfloat16),
            pltpu.VMEM(lanes.shape, jnp.int32),
            pltpu.SemaphoreType.DMA(()),
            pltpu.SemaphoreType.DMA(()),
        ],
        compiler_params=pltpu.CompilerParams(vmem_limit_bytes=4 << 20),
        name="pick",
    )(local, spectra, lanes)


def times_root(re, im):
    return (re - im) * ROOT, (re + im) * ROOT


def four(x):
    (ar, ai), (br, bi), (cr, ci), (dr, di) = x
    sr, si, tr, ti = ar + cr, ai + ci, ar - cr, ai - ci
    ur, ui, vr, vi = br + dr, bi + di, br - dr, bi - di
    return [(sr + ur, si + ui), (tr - vi, ti + vr), (sr - ur, si - ui), (tr + vi, ti - vr)]


def lags_kernel(base, values_ref, slab_ref, twiddle_ref, high_ref, low_ref, out_ref, hi_ref, lo_ref, acc_ref):
    chans = out_ref.shape[1]
    segs = values_ref.shape[1]
    steps = SPAN // LANES

    def produce(n, slot):
        def at(j):
            return pl.ds(pl.multiple_of(j * SPAN + n * LANES, LANES), LANES)

        for r in range(0, chans, ROWS):
            x = []
            for j in range(RES // 2):
                re = im = None
                for g in range(segs):
                    vr = values_ref[0, g, pl.ds(base + r, ROWS), at(j)].astype(jnp.float32)
                    vi = values_ref[1, g, pl.ds(base + r, ROWS), at(j)].astype(jnp.float32)
                    sr = slab_ref[pl.ds(g, 1), at(j)]
                    si = slab_ref[pl.ds(segs + g, 1), at(j)]
                    pr = sr * vr + si * vi
                    pi = sr * vi - si * vr
                    re = pr if re is None else re + pr
                    im = pi if im is None else im + pi
                x.append((re, im))
            even = four(x)
            (br, bi), (dr, di) = x[1], x[3]
            odd = four(
                [
                    x[0],
                    times_root(br, bi),
                    (-x[2][1], x[2][0]),
                    ((-dr - di) * ROOT, (dr - di) * ROOT),
                ]
            )
            for u in range(RES):
                gr, gi = even[u // 2] if u % 2 == 0 else odd[u // 2]
                if u:
                    cos = twiddle_ref[pl.ds(2 * u, 1), at(0)]
                    sin = twiddle_ref[pl.ds(2 * u + 1, 1), at(0)]
                    gr, gi = gr * cos - gi * sin, gr * sin + gi * cos
                for k, part in enumerate((gr, gi)):
                    top = part.astype(jnp.bfloat16)
                    rest = (part - top.astype(jnp.float32)).astype(jnp.bfloat16)
                    where = (slot, pl.ds(u * chans + r, ROWS), pl.ds(k * LANES, LANES))
                    hi_ref[where] = top
                    lo_ref[where] = rest

    def contract(n, slot):
        rows = pl.ds(pl.multiple_of(n * 2 * LANES, 2 * LANES), 2 * LANES)
        whi = high_ref[rows, :]
        hi = hi_ref[slot]
        dot = lambda a, b: jnp.dot(a, b, preferred_element_type=jnp.float32)
        return dot(hi, whi) + dot(lo_ref[slot], whi) + dot(hi, low_ref[rows, :])

    produce(0, 0)
    acc_ref[...] = jnp.zeros_like(acc_ref)

    def step(n, carry):
        produce(n, n % 2)
        acc_ref[...] += contract(n - 1, (n - 1) % 2)
        return carry

    lax.fori_loop(1, steps, step, 0)
    acc_ref[...] += contract(steps - 1, (steps - 1) % 2)

    piece = COLS // RES
    per = LANES // piece
    lane = lax.broadcasted_iota(jnp.int32, (8, LANES), 1)
    for r in range(0, chans, 8):
        turned = []
        for u in range(RES):
            halves = [acc_ref[pl.ds(u * chans + r, 8), pl.ds(h * LANES, LANES)] for h in range(2)]
            shift = piece * u
            if shift >= LANES:
                halves = halves[::-1]
                shift -= LANES
            if shift:
                a, b = (pltpu.roll(x, shift, 1) for x in halves)
                head = lane < shift
                halves = [jnp.where(head, b, a), jnp.where(head, a, b)]
            turned.append(halves)
        for w in range(RES):
            for h in range(2):
                picks = [turned[(h * per + s - w) % RES][h] for s in range(per)]
                left = jnp.where(lane < piece, picks[0], picks[1])
                right = jnp.where(lane < 3 * piece, picks[2], picks[3])
                out_ref[w, pl.ds(r, 8), pl.ds(h * LANES, LANES)] = jnp.where(lane < 2 * piece, left, right)


def partial_lags(values, slab, tabs, base, chans):
    high, low, twiddle = tabs
    vmem = pl.BlockSpec(memory_space=pltpu.VMEM)
    return pl.pallas_call(
        lambda *refs: lags_kernel(base, *refs),
        in_specs=[vmem] * 5,
        out_specs=vmem,
        out_shape=jax.ShapeDtypeStruct((RES, chans, COLS), jnp.float32),
        scratch_shapes=[
            pltpu.VMEM((2, RES * chans, 2 * LANES), jnp.bfloat16),
            pltpu.VMEM((2, RES * chans, 2 * LANES), jnp.bfloat16),
            pltpu.VMEM((RES * chans, COLS), jnp.float32),
        ],
        compiler_params=pltpu.CompilerParams(vmem_limit_bytes=16 << 20),
        name="lags",
    )(values, slab, twiddle, high, low)


def finish_kernel(own_ref, tiles_ref, out_ref):
    total = tiles_ref[0]
    for peer in range(1, tiles_ref.shape[0]):
        total = total + tiles_ref[peer]
    piece = COLS // RES
    place = lax.broadcasted_iota(jnp.int32, (COLS, COLS), 0)
    lag = lax.broadcasted_iota(jnp.int32, (COLS, COLS), 1)
    residue = (place // piece - own_ref[0] + RES) % RES
    order = jnp.where(lag == place % piece * RES + residue, 1.0, 0.0).astype(jnp.bfloat16)
    first = total.astype(jnp.bfloat16)
    rest = total - first.astype(jnp.float32)
    second = rest.astype(jnp.bfloat16)
    third = (rest - second.astype(jnp.float32)).astype(jnp.bfloat16)
    dot = lambda a: jnp.dot(a, order, preferred_element_type=jnp.float32)
    out_ref[...] = (dot(third) + dot(second)) + dot(first)


def finish(own, tiles):
    return pl.pallas_call(
        finish_kernel,
        in_specs=[pl.BlockSpec(memory_space=pltpu.SMEM), pl.BlockSpec(memory_space=pltpu.VMEM)],
        out_specs=pl.BlockSpec(memory_space=pltpu.VMEM),
        out_shape=jax.ShapeDtypeStruct(tiles.shape[1:], jnp.float32),
        compiler_params=pltpu.CompilerParams(vmem_limit_bytes=8 << 20),
        name="finish",
    )(own, tiles)


def spread(slab):
    peers = lax.axis_size("chan")
    for bit in (1, 16, 2, 4, 8):
        slab = slab + lax.ppermute(slab, "chan", [(peer, peer ^ bit) for peer in range(peers)])
    return slab


def body(spectra, exponents, source_channels):
    chans = spectra.shape[2]
    segs = spectra.shape[1] * lax.axis_size("win")
    stay = lambda array: pltpu.with_memory_space_constraint(array, pltpu.MemorySpace.HBM)
    spectra = stay(spectra)
    lanes = stay(jnp.transpose(exponents, (0, 2, 1)))
    local = source_channels - lax.axis_index("chan") * chans
    slab = spread(pick(local, spectra, lanes))
    values = dequantize(spectra, lanes)
    tabs = tables(1.0 / math.sqrt(4.0 * F * segs))
    partial = partial_lags(values, slab, tabs, 0, chans)
    tiles = lax.all_to_all(partial, "win", 0, 0, tiled=True)
    own = lax.axis_index("win").reshape(1).astype(jnp.int32)
    return finish(own, tiles)[None]


def solution(mesh):
    return jax.shard_map(
        body,
        mesh=mesh,
        in_specs=(P(None, "win", "chan", None), P("win", "chan", None), P()),
        out_specs=P(None, "chan", "win"),
        check_vma=False,
    )
```

```python
import math

import jax
import jax.numpy as jnp
import numpy as np
from jax import lax
from jax.experimental import pallas as pl
from jax.experimental.pallas import tpu as pltpu
from jax.sharding import PartitionSpec as P

F = 4096
L = 2048
RES = 8
SPAN = 2 * F // RES
COLS = L // RES
LANES = 128
ROWS = 16
PIECE = 32
ROOT = math.sqrt(0.5)


def tables(norm):
    bins = np.arange(SPAN)
    lag = np.arange(COLS) - COLS // 2
    angle = 2.0 * np.pi * ((bins[:, None] * lag[None, :]) % SPAN) / SPAN
    parts = np.stack([np.cos(angle), -np.sin(angle)], 0) * norm
    parts = parts.reshape(2, SPAN // LANES, LANES, COLS).transpose(1, 0, 2, 3)
    whole = parts.reshape(2 * SPAN, COLS)
    high = whole.astype(jnp.bfloat16)
    low = (whole - high.astype(np.float64)).astype(jnp.bfloat16)
    turn = 2.0 * np.pi * (np.arange(RES)[:, None] * bins[None, :]) / (2 * F)
    twiddle = np.stack([np.cos(turn), np.sin(turn)], 1).reshape(2 * RES, SPAN)
    return high, low, twiddle.astype(np.float32)


def dequantize_kernel(codes_ref, exponents_ref, values_ref):
    seg, part = pl.program_id(0), pl.program_id(1)
    scale = jnp.exp2(exponents_ref[0].astype(jnp.float32)).T
    for block in range(scale.shape[1]):
        wide = jnp.broadcast_to(scale[:, block : block + 1], (scale.shape[0], LANES))
        wide = wide.astype(jnp.bfloat16).astype(jnp.float32)
        at = pl.ds(block * LANES, LANES)
        values_ref[part, seg, :, at] = codes_ref[0, 0, :, at].astype(jnp.float32) * wide


def dequantize(spectra, lanes):
    _, segs, chans, nbin = spectra.shape
    return pl.pallas_call(
        dequantize_kernel,
        grid=(segs, 2),
        in_specs=[
            pl.BlockSpec((1, 1, chans, nbin), lambda g, p: (p, g, 0, 0)),
            pl.BlockSpec((1, lanes.shape[1], chans), lambda g, p: (g, 0, 0)),
        ],
        out_specs=pl.BlockSpec(memory_space=pltpu.VMEM),
        out_shape=jax.ShapeDtypeStruct(spectra.shape, jnp.float32),
        compiler_params=pltpu.CompilerParams(vmem_limit_bytes=20 << 20),
        name="dequantize",
    )(spectra, lanes)


def pick_kernel(local_ref, codes_ref, exponents_ref, slab_ref, rows_ref, lanes_ref, row_sem, lane_sem):
    segs, blocks, chans = lanes_ref.shape
    local = local_ref[0]
    owned = (local >= 0) & (local < chans)
    row = jnp.clip(local, 0, chans - 1)
    first = pl.multiple_of(row // ROWS * ROWS, ROWS)
    rows_in = pltpu.make_async_copy(codes_ref.at[:, :, pl.ds(first, ROWS), :], rows_ref, row_sem)
    lanes_in = pltpu.make_async_copy(exponents_ref, lanes_ref, lane_sem)
    rows_in.start()
    lanes_in.start()
    own_lane = lax.broadcasted_iota(jnp.int32, (blocks, chans), 1) == row
    own_row = lax.broadcasted_iota(jnp.int32, (ROWS, LANES), 0) == row % ROWS
    lanes_in.wait()
    rows_in.wait()
    for g in range(segs):
        exponent = jnp.sum(jnp.where(own_lane, lanes_ref[g].astype(jnp.float32), 0.0), axis=1, keepdims=True)
        scale = jnp.where(owned, jnp.exp2(exponent), 0.0)
        scale = jnp.broadcast_to(scale, (blocks, LANES)).astype(jnp.bfloat16).astype(jnp.float32)
        for part in range(2):
            for block in range(blocks):
                at = pl.ds(block * LANES, LANES)
                codes = rows_ref[part, g, :, at].astype(jnp.float32)
                code = jnp.sum(jnp.where(own_row, codes, 0.0), axis=0, keepdims=True)
                slab_ref[pl.ds(part * segs + g, 1), at] = code * scale[block : block + 1]


def pick(local, spectra, lanes):
    _, segs, _, nbin = spectra.shape
    hbm = pl.BlockSpec(memory_space=pltpu.MemorySpace.HBM)
    return pl.pallas_call(
        pick_kernel,
        in_specs=[pl.BlockSpec(memory_space=pltpu.SMEM), hbm, hbm],
        out_specs=pl.BlockSpec(memory_space=pltpu.VMEM),
        out_shape=jax.ShapeDtypeStruct((2 * segs, nbin), jnp.float32),
        scratch_shapes=[
            pltpu.VMEM((2, segs, ROWS, nbin), jnp.bfloat16),
            pltpu.VMEM(lanes.shape, jnp.int32),
            pltpu.SemaphoreType.DMA(()),
            pltpu.SemaphoreType.DMA(()),
        ],
        compiler_params=pltpu.CompilerParams(vmem_limit_bytes=4 << 20),
        name="pick",
    )(local, spectra, lanes)


def times_root(re, im):
    return (re - im) * ROOT, (re + im) * ROOT


def four(x):
    (ar, ai), (br, bi), (cr, ci), (dr, di) = x
    sr, si, tr, ti = ar + cr, ai + ci, ar - cr, ai - ci
    ur, ui, vr, vi = br + dr, bi + di, br - dr, bi - di
    return [(sr + ur, si + ui), (tr - vi, ti + vr), (sr - ur, si - ui), (tr + vi, ti - vr)]


def lags_kernel(values_ref, slab_ref, twiddle_ref, high_ref, low_ref, out_ref, acc_ref, *parts):
    chans = out_ref.shape[1]
    segs = values_ref.shape[1]
    steps = SPAN // LANES
    tall = RES * ROWS
    slots = (parts[:4], parts[4:])

    def produce(n, slot, begin=0, end=chans):
        def at(j):
            return pl.ds(pl.multiple_of(j * SPAN + n * LANES, LANES), LANES)

        for r in range(begin, end, ROWS):
            x = []
            for j in range(RES // 2):
                re = im = None
                for g in range(segs):
                    vr = values_ref[0, g, pl.ds(r, ROWS), at(j)]
                    vi = values_ref[1, g, pl.ds(r, ROWS), at(j)]
                    sr = slab_ref[pl.ds(g, 1), at(j)]
                    si = slab_ref[pl.ds(segs + g, 1), at(j)]
                    pr = sr * vr + si * vi
                    pi = sr * vi - si * vr
                    re = pr if re is None else re + pr
                    im = pi if im is None else im + pi
                x.append((re, im))
            even = four(x)
            (br, bi), (dr, di) = x[1], x[3]
            odd = four(
                [
                    x[0],
                    times_root(br, bi),
                    (-x[2][1], x[2][0]),
                    ((-dr - di) * ROOT, (dr - di) * ROOT),
                ]
            )
            for u in range(RES):
                gr, gi = even[u // 2] if u % 2 == 0 else odd[u // 2]
                if u:
                    cos = twiddle_ref[pl.ds(2 * u, 1), at(0)]
                    sin = twiddle_ref[pl.ds(2 * u + 1, 1), at(0)]
                    gr, gi = gr * cos - gi * sin, gr * sin + gi * cos
                rows = pl.ds(r * RES + u * ROWS, ROWS)
                for k, part in enumerate((gr, gi)):
                    top = part.astype(jnp.bfloat16)
                    slots[slot][k][rows, :] = top
                    slots[slot][2 + k][rows, :] = (part - top.astype(jnp.float32)).astype(jnp.bfloat16)

    def contract(n, slot, begin=0, end=chans):
        piece = pl.ds(begin * RES, (end - begin) * RES)
        rows = pl.ds(pl.multiple_of(n * 2 * LANES, 2 * LANES), 2 * LANES)
        table = jnp.concatenate([high_ref[rows, :], high_ref[rows, :], low_ref[rows, :]], axis=0)
        hr, hi, lr, li = (ref[piece, :] for ref in slots[slot])
        both = jnp.concatenate([hr, hi, lr, li, hr, hi], axis=1)
        acc_ref[piece, :] += jnp.dot(both, table, preferred_element_type=jnp.float32)

    acc_ref[...] = jnp.zeros_like(acc_ref)
    produce(0, 0)

    def step(n, carry):
        for slot in range(2):

            @pl.when(n % 2 == slot)
            def _():
                for begin in range(0, chans, PIECE):
                    contract(n - 1, 1 - slot, begin, begin + PIECE)
                    produce(n, slot, begin, begin + PIECE)

        return carry

    lax.fori_loop(1, steps, step, 0)
    piece = COLS // RES
    per = LANES // piece
    lane = lax.broadcasted_iota(jnp.int32, (8, LANES), 1)
    for begin in range(0, chans, PIECE):
        contract(steps - 1, (steps - 1) % 2, begin, begin + PIECE)
        for r in range(begin, begin + PIECE, 8):
            turned = []
            for u in range(RES):
                rows = pl.ds(r // ROWS * tall + u * ROWS + r % ROWS, 8)
                halves = [acc_ref[rows, pl.ds(h * LANES, LANES)] for h in range(2)]
                shift = piece * u
                if shift >= LANES:
                    halves = halves[::-1]
                    shift -= LANES
                if shift:
                    a, b = (pltpu.roll(x, shift, 1) for x in halves)
                    head = lane < shift
                    halves = [jnp.where(head, b, a), jnp.where(head, a, b)]
                turned.append(halves)
            for w in range(RES):
                for h in range(2):
                    picks = [turned[(h * per + s - w) % RES][h] for s in range(per)]
                    left = jnp.where(lane < piece, picks[0], picks[1])
                    right = jnp.where(lane < 3 * piece, picks[2], picks[3])
                    out_ref[w, pl.ds(r, 8), pl.ds(h * LANES, LANES)] = jnp.where(lane < 2 * piece, left, right)


def partial_lags(values, slab, tabs):
    chans = values.shape[2]
    high, low, twiddle = tabs
    vmem = pl.BlockSpec(memory_space=pltpu.VMEM)
    return pl.pallas_call(
        lags_kernel,
        in_specs=[vmem] * 5,
        out_specs=vmem,
        out_shape=jax.ShapeDtypeStruct((RES, chans, COLS), jnp.float32),
        scratch_shapes=[pltpu.VMEM((RES * chans, COLS), jnp.float32)]
        + [pltpu.VMEM((RES * chans, LANES), jnp.bfloat16)] * 8,
        compiler_params=pltpu.CompilerParams(vmem_limit_bytes=16 << 20),
        name="lags",
    )(values, slab, twiddle, high, low)


def finish_kernel(own_ref, tiles_ref, out_ref):
    total = tiles_ref[0]
    for peer in range(1, tiles_ref.shape[0]):
        total = total + tiles_ref[peer]
    piece = COLS // RES
    place = lax.broadcasted_iota(jnp.int32, (COLS, COLS), 0)
    lag = lax.broadcasted_iota(jnp.int32, (COLS, COLS), 1)
    residue = (place // piece - own_ref[0] + RES) % RES
    order = jnp.where(lag == place % piece * RES + residue, 1.0, 0.0).astype(jnp.bfloat16)
    first = total.astype(jnp.bfloat16)
    rest = total - first.astype(jnp.float32)
    second = rest.astype(jnp.bfloat16)
    third = (rest - second.astype(jnp.float32)).astype(jnp.bfloat16)
    dot = lambda a: jnp.dot(a, order, preferred_element_type=jnp.float32)
    out_ref[...] = (dot(third) + dot(second)) + dot(first)


def finish(own, tiles):
    return pl.pallas_call(
        finish_kernel,
        in_specs=[pl.BlockSpec(memory_space=pltpu.SMEM), pl.BlockSpec(memory_space=pltpu.VMEM)],
        out_specs=pl.BlockSpec(memory_space=pltpu.VMEM),
        out_shape=jax.ShapeDtypeStruct(tiles.shape[1:], jnp.float32),
        compiler_params=pltpu.CompilerParams(vmem_limit_bytes=8 << 20),
        name="finish",
    )(own, tiles)


def spread(slab):
    peers = lax.axis_size("chan")
    for bit in (1, 16, 2, 4, 12):
        slab = slab + lax.ppermute(slab, "chan", [(peer, peer ^ bit) for peer in range(peers)])
    return slab


def body(spectra, exponents, source_channels):
    chans = spectra.shape[2]
    segs = spectra.shape[1] * lax.axis_size("win")
    stay = lambda array: pltpu.with_memory_space_constraint(array, pltpu.MemorySpace.HBM)
    spectra = stay(spectra)
    lanes = stay(jnp.transpose(exponents, (0, 2, 1)))
    local = source_channels - lax.axis_index("chan") * chans
    slab = spread(pick(local, spectra, lanes))
    values = dequantize(spectra, lanes)
    tabs = tables(1.0 / math.sqrt(4.0 * F * segs))
    partial = partial_lags(values, slab, tabs)
    tiles = lax.all_to_all(partial, "win", 0, 0, tiled=True)
    own = lax.axis_index("win").reshape(1).astype(jnp.int32)
    return finish(own, tiles)[None]


def solution(mesh):
    return jax.shard_map(
        body,
        mesh=mesh,
        in_specs=(P(None, "win", "chan", None), P("win", "chan", None), P()),
        out_specs=P(None, "chan", "win"),
        check_vma=False,
    )
```

```python
import math

import jax
import jax.numpy as jnp
import numpy as np
from jax import lax
from jax.experimental import pallas as pl
from jax.experimental.pallas import tpu as pltpu
from jax.sharding import PartitionSpec as P

F = 4096
L = 2048
RES = 8
SPAN = 2 * F // RES
COLS = L // RES
LANES = 128
ROWS = 16
PIECE = 32
ROOT = math.sqrt(0.5)


def tables(norm):
    bins = np.arange(SPAN)
    lag = np.arange(COLS) - COLS // 2
    angle = 2.0 * np.pi * ((bins[:, None] * lag[None, :]) % SPAN) / SPAN
    parts = np.stack([np.cos(angle), -np.sin(angle)], 0) * norm
    parts = parts.reshape(2, SPAN // LANES, LANES, COLS).transpose(1, 0, 2, 3)
    whole = parts.reshape(2 * SPAN, COLS)
    high = whole.astype(jnp.bfloat16)
    low = (whole - high.astype(np.float64)).astype(jnp.bfloat16)
    turn = 2.0 * np.pi * (np.arange(RES)[:, None] * bins[None, :]) / (2 * F)
    twiddle = np.stack([np.cos(turn), np.sin(turn)], 1).reshape(2 * RES, SPAN)
    return high, low, twiddle.astype(np.float32)


def dequantize_kernel(codes_ref, exponents_ref, values_ref):
    seg, cut = pl.program_id(0), pl.program_id(1)
    _, blocks, chans = exponents_ref.shape
    scale = jnp.exp2(exponents_ref[0].astype(jnp.float32)).T
    scale = scale.astype(jnp.bfloat16).astype(jnp.float32)
    for block in range(blocks):
        wide = jnp.broadcast_to(scale[:, block : block + 1], (chans, LANES))
        at = pl.ds(block * LANES, LANES)
        to = pl.ds(pl.multiple_of((cut * blocks + block) * LANES, LANES), LANES)
        for part in range(2):
            values_ref[part, seg, :, to] = codes_ref[part, 0, :, at].astype(jnp.float32) * wide


def dequantize(spectra, lanes):
    _, segs, chans, nbin = spectra.shape
    cuts = 4
    return pl.pallas_call(
        dequantize_kernel,
        grid=(segs, cuts),
        in_specs=[
            pl.BlockSpec((2, 1, chans, nbin // cuts), lambda g, k: (0, g, 0, k)),
            pl.BlockSpec((1, lanes.shape[1] // cuts, chans), lambda g, k: (g, k, 0)),
        ],
        out_specs=pl.BlockSpec(memory_space=pltpu.VMEM),
        out_shape=jax.ShapeDtypeStruct(spectra.shape, jnp.float32),
        compiler_params=pltpu.CompilerParams(vmem_limit_bytes=20 << 20),
        name="dequantize",
    )(spectra, lanes)


def pick_kernel(source_ref, codes_ref, exponents_ref, slab_ref, rows_ref, lanes_ref, row_sem, lane_sem):
    segs, blocks, chans = lanes_ref.shape
    local = source_ref[0] - lax.axis_index("chan") * chans
    owned = (local >= 0) & (local < chans)
    row = jnp.clip(local, 0, chans - 1)
    first = pl.multiple_of(row // ROWS * ROWS, ROWS)
    rows_in = pltpu.make_async_copy(codes_ref.at[:, :, pl.ds(first, ROWS), :], rows_ref, row_sem)
    lanes_in = pltpu.make_async_copy(exponents_ref, lanes_ref, lane_sem)
    rows_in.start()
    lanes_in.start()
    own_lane = lax.broadcasted_iota(jnp.int32, (blocks, chans), 1) == row
    own_row = lax.broadcasted_iota(jnp.int32, (ROWS, LANES), 0) == row % ROWS
    lanes_in.wait()
    rows_in.wait()
    for g in range(segs):
        exponent = jnp.sum(jnp.where(own_lane, lanes_ref[g].astype(jnp.float32), 0.0), axis=1, keepdims=True)
        scale = jnp.where(owned, jnp.exp2(exponent), 0.0)
        scale = jnp.broadcast_to(scale, (blocks, LANES)).astype(jnp.bfloat16).astype(jnp.float32)
        for part in range(2):
            for block in range(blocks):
                at = pl.ds(block * LANES, LANES)
                codes = rows_ref[part, g, :, at].astype(jnp.float32)
                code = jnp.sum(jnp.where(own_row, codes, 0.0), axis=0, keepdims=True)
                slab_ref[pl.ds(part * segs + g, 1), at] = code * scale[block : block + 1]


def pick(source_channels, spectra, lanes):
    _, segs, _, nbin = spectra.shape
    hbm = pl.BlockSpec(memory_space=pltpu.MemorySpace.HBM)
    return pl.pallas_call(
        pick_kernel,
        in_specs=[pl.BlockSpec(memory_space=pltpu.SMEM), hbm, hbm],
        out_specs=pl.BlockSpec(memory_space=pltpu.VMEM),
        out_shape=jax.ShapeDtypeStruct((2 * segs, nbin), jnp.float32),
        scratch_shapes=[
            pltpu.VMEM((2, segs, ROWS, nbin), jnp.bfloat16),
            pltpu.VMEM(lanes.shape, jnp.int32),
            pltpu.SemaphoreType.DMA(()),
            pltpu.SemaphoreType.DMA(()),
        ],
        compiler_params=pltpu.CompilerParams(vmem_limit_bytes=4 << 20),
        name="pick",
    )(source_channels, spectra, lanes)


def times_root(re, im):
    return (re - im) * ROOT, (re + im) * ROOT


def four(x):
    (ar, ai), (br, bi), (cr, ci), (dr, di) = x
    sr, si, tr, ti = ar + cr, ai + ci, ar - cr, ai - ci
    ur, ui, vr, vi = br + dr, bi + di, br - dr, bi - di
    return [(sr + ur, si + ui), (tr - vi, ti + vr), (sr - ur, si - ui), (tr + vi, ti - vr)]


def lags_kernel(values_ref, slab_ref, twiddle_ref, high_ref, low_ref, out_ref, acc_ref, *parts):
    chans = out_ref.shape[1]
    segs = values_ref.shape[1]
    steps = SPAN // LANES
    tall = RES * ROWS
    slots = (parts[:4], parts[4:])

    def produce(n, slot, begin=0, end=chans):
        def at(j):
            return pl.ds(pl.multiple_of(j * SPAN + n * LANES, LANES), LANES)

        for r in range(begin, end, ROWS):
            x = []
            for j in range(RES // 2):
                re = im = None
                for g in range(segs):
                    vr = values_ref[0, g, pl.ds(r, ROWS), at(j)]
                    vi = values_ref[1, g, pl.ds(r, ROWS), at(j)]
                    sr = slab_ref[pl.ds(g, 1), at(j)]
                    si = slab_ref[pl.ds(segs + g, 1), at(j)]
                    pr = sr * vr + si * vi
                    pi = sr * vi - si * vr
                    re = pr if re is None else re + pr
                    im = pi if im is None else im + pi
                x.append((re, im))
            even = four(x)
            (br, bi), (dr, di) = x[1], x[3]
            odd = four(
                [
                    x[0],
                    times_root(br, bi),
                    (-x[2][1], x[2][0]),
                    ((-dr - di) * ROOT, (dr - di) * ROOT),
                ]
            )
            for u in range(RES):
                gr, gi = even[u // 2] if u % 2 == 0 else odd[u // 2]
                if u:
                    cos = twiddle_ref[pl.ds(2 * u, 1), at(0)]
                    sin = twiddle_ref[pl.ds(2 * u + 1, 1), at(0)]
                    gr, gi = gr * cos - gi * sin, gr * sin + gi * cos
                rows = pl.ds(r * RES + u * ROWS, ROWS)
                for k, part in enumerate((gr, gi)):
                    top = part.astype(jnp.bfloat16)
                    slots[slot][k][rows, :] = top
                    slots[slot][2 + k][rows, :] = (part - top.astype(jnp.float32)).astype(jnp.bfloat16)

    def contract(n, slot, begin=0, end=chans):
        piece = pl.ds(begin * RES, (end - begin) * RES)
        rows = pl.ds(pl.multiple_of(n * 2 * LANES, 2 * LANES), 2 * LANES)
        table = jnp.concatenate([high_ref[rows, :], high_ref[rows, :], low_ref[rows, :]], axis=0)
        hr, hi, lr, li = (ref[piece, :] for ref in slots[slot])
        both = jnp.concatenate([hr, hi, lr, li, hr, hi], axis=1)
        acc_ref[piece, :] += jnp.dot(both, table, preferred_element_type=jnp.float32)

    acc_ref[...] = jnp.zeros_like(acc_ref)
    produce(0, 0)

    def step(n, carry):
        for slot in range(2):

            @pl.when(n % 2 == slot)
            def _():
                for begin in range(0, chans, PIECE):
                    contract(n - 1, 1 - slot, begin, begin + PIECE)
                    produce(n, slot, begin, begin + PIECE)

        return carry

    lax.fori_loop(1, steps, step, 0)
    piece = COLS // RES
    per = LANES // piece
    lane = lax.broadcasted_iota(jnp.int32, (8, LANES), 1)
    for begin in range(0, chans, PIECE):
        contract(steps - 1, (steps - 1) % 2, begin, begin + PIECE)
        for r in range(begin, begin + PIECE, 8):
            turned = []
            for u in range(RES):
                rows = pl.ds(r // ROWS * tall + u * ROWS + r % ROWS, 8)
                halves = [acc_ref[rows, pl.ds(h * LANES, LANES)] for h in range(2)]
                shift = piece * u
                if shift >= LANES:
                    halves = halves[::-1]
                    shift -= LANES
                if shift:
                    a, b = (pltpu.roll(x, shift, 1) for x in halves)
                    head = lane < shift
                    halves = [jnp.where(head, b, a), jnp.where(head, a, b)]
                turned.append(halves)
            for w in range(RES):
                for h in range(2):
                    picks = [turned[(h * per + s - w) % RES][h] for s in range(per)]
                    left = jnp.where(lane < piece, picks[0], picks[1])
                    right = jnp.where(lane < 3 * piece, picks[2], picks[3])
                    out_ref[w, pl.ds(r, 8), pl.ds(h * LANES, LANES)] = jnp.where(lane < 2 * piece, left, right)


def partial_lags(values, slab, tabs):
    chans = values.shape[2]
    high, low, twiddle = tabs
    vmem = pl.BlockSpec(memory_space=pltpu.VMEM)
    return pl.pallas_call(
        lags_kernel,
        in_specs=[vmem] * 5,
        out_specs=vmem,
        out_shape=jax.ShapeDtypeStruct((RES, chans, COLS), jnp.float32),
        scratch_shapes=[pltpu.VMEM((RES * chans, COLS), jnp.float32)]
        + [pltpu.VMEM((RES * chans, LANES), jnp.bfloat16)] * 8,
        compiler_params=pltpu.CompilerParams(vmem_limit_bytes=16 << 20),
        name="lags",
    )(values, slab, twiddle, high, low)


def finish_kernel(tiles_ref, out_ref):
    total = tiles_ref[0]
    for peer in range(1, tiles_ref.shape[0]):
        total = total + tiles_ref[peer]
    piece = COLS // RES
    place = lax.broadcasted_iota(jnp.int32, (COLS, COLS), 0)
    lag = lax.broadcasted_iota(jnp.int32, (COLS, COLS), 1)
    residue = (place // piece - lax.axis_index("win") + RES) % RES
    order = jnp.where(lag == place % piece * RES + residue, 1.0, 0.0).astype(jnp.bfloat16)
    first = total.astype(jnp.bfloat16)
    rest = total - first.astype(jnp.float32)
    second = rest.astype(jnp.bfloat16)
    third = (rest - second.astype(jnp.float32)).astype(jnp.bfloat16)
    dot = lambda a: jnp.dot(a, order, preferred_element_type=jnp.float32)
    out_ref[...] = (dot(third) + dot(second)) + dot(first)


def finish(tiles):
    return pl.pallas_call(
        finish_kernel,
        in_specs=[pl.BlockSpec(memory_space=pltpu.VMEM)],
        out_specs=pl.BlockSpec(memory_space=pltpu.VMEM),
        out_shape=jax.ShapeDtypeStruct(tiles.shape[1:], jnp.float32),
        compiler_params=pltpu.CompilerParams(vmem_limit_bytes=8 << 20),
        name="finish",
    )(tiles)


def spread(slab):
    peers = lax.axis_size("chan")
    for bit in (1, 16, 2, 4, 12):
        slab = slab + lax.ppermute(slab, "chan", [(peer, peer ^ bit) for peer in range(peers)])
    return slab


def body(spectra, exponents, source_channels):
    segs = spectra.shape[1] * lax.axis_size("win")
    stay = lambda array: pltpu.with_memory_space_constraint(array, pltpu.MemorySpace.HBM)
    spectra = stay(spectra)
    lanes = stay(jnp.transpose(exponents, (0, 2, 1)))
    slab = spread(pick(source_channels, spectra, lanes))
    values = dequantize(spectra, lanes)
    tabs = tables(1.0 / math.sqrt(4.0 * F * segs))
    partial = partial_lags(values, slab, tabs)
    return finish(lax.all_to_all(partial, "win", 0, 0, tiled=True))[None]


def solution(mesh):
    return jax.shard_map(
        body,
        mesh=mesh,
        in_specs=(P(None, "win", "chan", None), P("win", "chan", None), P()),
        out_specs=P(None, "chan", "win"),
        check_vma=False,
    )
```

```python
import math

import jax
import jax.numpy as jnp
import numpy as np
from jax import lax
from jax.experimental import pallas as pl
from jax.experimental.pallas import tpu as pltpu
from jax.sharding import PartitionSpec as P

F = 4096
L = 2048
RES = 8
SPAN = 2 * F // RES
COLS = L // RES
LANES = 128
ROWS = 16
PIECE = 32
ROOT = math.sqrt(0.5)


def tables(norm):
    bins = np.arange(SPAN)
    lag = np.arange(COLS) - COLS // 2
    angle = 2.0 * np.pi * ((bins[:, None] * lag[None, :]) % SPAN) / SPAN
    parts = np.stack([np.cos(angle), -np.sin(angle)], 0) * norm
    parts = parts.reshape(2, SPAN // LANES, LANES, COLS).transpose(1, 0, 2, 3)
    whole = parts.reshape(2 * SPAN, COLS)
    high = whole.astype(jnp.bfloat16)
    low = (whole - high.astype(np.float64)).astype(jnp.bfloat16)
    turn = 2.0 * np.pi * (np.arange(RES)[:, None] * bins[None, :]) / (2 * F)
    twiddle = np.stack([np.cos(turn), np.sin(turn)], 1).reshape(2 * RES, SPAN)
    return high, low, twiddle.astype(np.float32)


def dequantize_kernel(codes_ref, exponents_ref, values_ref):
    part = pl.program_id(0)
    _, blocks, chans = exponents_ref.shape
    scale = jnp.exp2(exponents_ref[0].astype(jnp.float32)).T
    scale = scale.astype(jnp.bfloat16).astype(jnp.float32)
    for block in range(blocks):
        wide = jnp.broadcast_to(scale[:, block : block + 1], (chans, LANES))
        at = pl.ds(block * LANES, LANES)
        values_ref[part, :, at] = codes_ref[0, 0, :, at].astype(jnp.float32) * wide


def dequantize(spectra, lanes, seg):
    _, _, chans, nbin = spectra.shape
    return pl.pallas_call(
        dequantize_kernel,
        grid=(2,),
        in_specs=[
            pl.BlockSpec((1, 1, chans, nbin), lambda p: (p, seg, 0, 0)),
            pl.BlockSpec((1, *lanes.shape[1:]), lambda p: (seg, 0, 0)),
        ],
        out_specs=pl.BlockSpec(memory_space=pltpu.VMEM),
        out_shape=jax.ShapeDtypeStruct((2, chans, nbin), jnp.float32),
        compiler_params=pltpu.CompilerParams(vmem_limit_bytes=8 << 20),
        name="dequantize",
    )(spectra, lanes)


def pick_kernel(source_ref, codes_ref, exponents_ref, slab_ref, rows_ref, lanes_ref, row_sem, lane_sem):
    segs, blocks, chans = lanes_ref.shape
    local = source_ref[0] - lax.axis_index("chan") * chans
    owned = (local >= 0) & (local < chans)
    row = jnp.clip(local, 0, chans - 1)
    first = pl.multiple_of(row // ROWS * ROWS, ROWS)
    rows_in = pltpu.make_async_copy(codes_ref.at[:, :, pl.ds(first, ROWS), :], rows_ref, row_sem)
    lanes_in = pltpu.make_async_copy(exponents_ref, lanes_ref, lane_sem)
    rows_in.start()
    lanes_in.start()
    own_lane = lax.broadcasted_iota(jnp.int32, (blocks, chans), 1) == row
    own_row = lax.broadcasted_iota(jnp.int32, (ROWS, LANES), 0) == row % ROWS
    lanes_in.wait()
    rows_in.wait()
    for g in range(segs):
        exponent = jnp.sum(jnp.where(own_lane, lanes_ref[g].astype(jnp.float32), 0.0), axis=1, keepdims=True)
        scale = jnp.where(owned, jnp.exp2(exponent), 0.0)
        scale = jnp.broadcast_to(scale, (blocks, LANES)).astype(jnp.bfloat16).astype(jnp.float32)
        for part in range(2):
            for block in range(blocks):
                at = pl.ds(block * LANES, LANES)
                codes = rows_ref[part, g, :, at].astype(jnp.float32)
                code = jnp.sum(jnp.where(own_row, codes, 0.0), axis=0, keepdims=True)
                slab_ref[pl.ds(part * segs + g, 1), at] = code * scale[block : block + 1]


def pick(source_channels, spectra, lanes):
    _, segs, _, nbin = spectra.shape
    hbm = pl.BlockSpec(memory_space=pltpu.MemorySpace.HBM)
    return pl.pallas_call(
        pick_kernel,
        in_specs=[pl.BlockSpec(memory_space=pltpu.SMEM), hbm, hbm],
        out_specs=pl.BlockSpec(memory_space=pltpu.VMEM),
        out_shape=jax.ShapeDtypeStruct((2 * segs, nbin), jnp.float32),
        scratch_shapes=[
            pltpu.VMEM((2, segs, ROWS, nbin), jnp.bfloat16),
            pltpu.VMEM(lanes.shape, jnp.int32),
            pltpu.SemaphoreType.DMA(()),
            pltpu.SemaphoreType.DMA(()),
        ],
        compiler_params=pltpu.CompilerParams(vmem_limit_bytes=4 << 20),
        name="pick",
    )(source_channels, spectra, lanes)


def times_root(re, im):
    return (re - im) * ROOT, (re + im) * ROOT


def four(x):
    (ar, ai), (br, bi), (cr, ci), (dr, di) = x
    sr, si, tr, ti = ar + cr, ai + ci, ar - cr, ai - ci
    ur, ui, vr, vi = br + dr, bi + di, br - dr, bi - di
    return [(sr + ur, si + ui), (tr - vi, ti + vr), (sr - ur, si - ui), (tr + vi, ti - vr)]


def lags_kernel(first_ref, second_ref, slab_ref, twiddle_ref, high_ref, low_ref, out_ref, acc_ref, *parts):
    chans = out_ref.shape[1]
    values = (first_ref, second_ref)
    segs = len(values)
    steps = SPAN // LANES
    tall = RES * ROWS
    slots = (parts[:4], parts[4:])

    def produce(n, slot, begin=0, end=chans):
        def at(j):
            return pl.ds(pl.multiple_of(j * SPAN + n * LANES, LANES), LANES)

        for r in range(begin, end, ROWS):
            x = []
            for j in range(RES // 2):
                re = im = None
                for g in range(segs):
                    vr = values[g][0, pl.ds(r, ROWS), at(j)]
                    vi = values[g][1, pl.ds(r, ROWS), at(j)]
                    sr = slab_ref[pl.ds(g, 1), at(j)]
                    si = slab_ref[pl.ds(segs + g, 1), at(j)]
                    pr = sr * vr + si * vi
                    pi = sr * vi - si * vr
                    re = pr if re is None else re + pr
                    im = pi if im is None else im + pi
                x.append((re, im))
            even = four(x)
            (br, bi), (dr, di) = x[1], x[3]
            odd = four(
                [
                    x[0],
                    times_root(br, bi),
                    (-x[2][1], x[2][0]),
                    ((-dr - di) * ROOT, (dr - di) * ROOT),
                ]
            )
            for u in range(RES):
                gr, gi = even[u // 2] if u % 2 == 0 else odd[u // 2]
                if u:
                    cos = twiddle_ref[pl.ds(2 * u, 1), at(0)]
                    sin = twiddle_ref[pl.ds(2 * u + 1, 1), at(0)]
                    gr, gi = gr * cos - gi * sin, gr * sin + gi * cos
                rows = pl.ds(r * RES + u * ROWS, ROWS)
                for k, part in enumerate((gr, gi)):
                    top = part.astype(jnp.bfloat16)
                    slots[slot][k][rows, :] = top
                    slots[slot][2 + k][rows, :] = (part - top.astype(jnp.float32)).astype(jnp.bfloat16)

    def contract(n, slot, begin=0, end=chans):
        piece = pl.ds(begin * RES, (end - begin) * RES)
        rows = pl.ds(pl.multiple_of(n * 2 * LANES, 2 * LANES), 2 * LANES)
        table = jnp.concatenate([high_ref[rows, :], high_ref[rows, :], low_ref[rows, :]], axis=0)
        hr, hi, lr, li = (ref[piece, :] for ref in slots[slot])
        both = jnp.concatenate([hr, hi, lr, li, hr, hi], axis=1)
        acc_ref[piece, :] += jnp.dot(both, table, preferred_element_type=jnp.float32)

    acc_ref[...] = jnp.zeros_like(acc_ref)
    produce(0, 0)

    def step(n, carry):
        for slot in range(2):

            @pl.when(n % 2 == slot)
            def _():
                for begin in range(0, chans, PIECE):
                    contract(n - 1, 1 - slot, begin, begin + PIECE)
                    produce(n, slot, begin, begin + PIECE)

        return carry

    lax.fori_loop(1, steps, step, 0)
    piece = COLS // RES
    per = LANES // piece
    lane = lax.broadcasted_iota(jnp.int32, (8, LANES), 1)
    for begin in range(0, chans, PIECE):
        contract(steps - 1, (steps - 1) % 2, begin, begin + PIECE)
        for r in range(begin, begin + PIECE, 8):
            turned = []
            for u in range(RES):
                rows = pl.ds(r // ROWS * tall + u * ROWS + r % ROWS, 8)
                halves = [acc_ref[rows, pl.ds(h * LANES, LANES)] for h in range(2)]
                shift = piece * u
                if shift >= LANES:
                    halves = halves[::-1]
                    shift -= LANES
                if shift:
                    a, b = (pltpu.roll(x, shift, 1) for x in halves)
                    head = lane < shift
                    halves = [jnp.where(head, b, a), jnp.where(head, a, b)]
                turned.append(halves)
            for w in range(RES):
                for h in range(2):
                    picks = [turned[(h * per + s - w) % RES][h] for s in range(per)]
                    left = jnp.where(lane < piece, picks[0], picks[1])
                    right = jnp.where(lane < 3 * piece, picks[2], picks[3])
                    out_ref[w, pl.ds(r, 8), pl.ds(h * LANES, LANES)] = jnp.where(lane < 2 * piece, left, right)


def partial_lags(values, slab, tabs):
    chans = values[0].shape[1]
    high, low, twiddle = tabs
    vmem = pl.BlockSpec(memory_space=pltpu.VMEM)
    return pl.pallas_call(
        lags_kernel,
        in_specs=[vmem] * 6,
        out_specs=vmem,
        out_shape=jax.ShapeDtypeStruct((RES, chans, COLS), jnp.float32),
        scratch_shapes=[pltpu.VMEM((RES * chans, COLS), jnp.float32)]
        + [pltpu.VMEM((RES * chans, LANES), jnp.bfloat16)] * 8,
        compiler_params=pltpu.CompilerParams(vmem_limit_bytes=16 << 20),
        name="lags",
    )(*values, slab, twiddle, high, low)


def finish_kernel(tiles_ref, out_ref):
    total = tiles_ref[0]
    for peer in range(1, tiles_ref.shape[0]):
        total = total + tiles_ref[peer]
    piece = COLS // RES
    place = lax.broadcasted_iota(jnp.int32, (COLS, COLS), 0)
    lag = lax.broadcasted_iota(jnp.int32, (COLS, COLS), 1)
    residue = (place // piece - lax.axis_index("win") + RES) % RES
    order = jnp.where(lag == place % piece * RES + residue, 1.0, 0.0).astype(jnp.bfloat16)
    first = total.astype(jnp.bfloat16)
    rest = total - first.astype(jnp.float32)
    second = rest.astype(jnp.bfloat16)
    third = (rest - second.astype(jnp.float32)).astype(jnp.bfloat16)
    dot = lambda a: jnp.dot(a, order, preferred_element_type=jnp.float32)
    out_ref[...] = (dot(third) + dot(second)) + dot(first)


def finish(tiles):
    return pl.pallas_call(
        finish_kernel,
        in_specs=[pl.BlockSpec(memory_space=pltpu.VMEM)],
        out_specs=pl.BlockSpec(memory_space=pltpu.VMEM),
        out_shape=jax.ShapeDtypeStruct(tiles.shape[1:], jnp.float32),
        compiler_params=pltpu.CompilerParams(vmem_limit_bytes=8 << 20),
        name="finish",
    )(tiles)


def exchange(slab, bit):
    peers = lax.axis_size("chan")
    return slab + lax.ppermute(slab, "chan", [(peer, peer ^ bit) for peer in range(peers)])


def body(spectra, exponents, source_channels):
    segs = spectra.shape[1] * lax.axis_size("win")
    stay = lambda array: pltpu.with_memory_space_constraint(array, pltpu.MemorySpace.HBM)
    spectra = stay(spectra)
    lanes = stay(jnp.transpose(exponents, (0, 2, 1)))
    slab = exchange(pick(source_channels, spectra, lanes), 1)
    slab, first = lax.optimization_barrier((exchange(slab, 16), dequantize(spectra, lanes, 0)))
    slab = exchange(slab, 2)
    slab, second = lax.optimization_barrier((exchange(slab, 4), dequantize(spectra, lanes, 1)))
    slab = exchange(slab, 12)
    tabs = tables(1.0 / math.sqrt(4.0 * F * segs))
    partial = partial_lags((first, second), slab, tabs)
    return finish(lax.all_to_all(partial, "win", 0, 0, tiled=True))[None]


def solution(mesh):
    return jax.shard_map(
        body,
        mesh=mesh,
        in_specs=(P(None, "win", "chan", None), P("win", "chan", None), P()),
        out_specs=P(None, "chan", "win"),
        check_vma=False,
    )
```

```python
import functools
import math

import jax
import jax.numpy as jnp
import numpy as np
from jax import lax
from jax.experimental import pallas as pl
from jax.experimental.pallas import tpu as pltpu
from jax.sharding import PartitionSpec as P

F = 4096
L = 2048
RES = 8
SPAN = 2 * F // RES
COLS = L // RES
LANES = 128
ROWS = 16
PIECE = 32
EIGHT = 8
CORES = 2
ROOT = math.sqrt(0.5)


def tables(norm):
    bins = np.arange(SPAN)
    lag = np.arange(COLS) - COLS // 2
    angle = 2.0 * np.pi * ((bins[:, None] * lag[None, :]) % SPAN) / SPAN
    parts = np.stack([np.cos(angle), -np.sin(angle)], 0) * norm
    parts = parts.reshape(2, SPAN // LANES, LANES, COLS).transpose(1, 0, 2, 3)
    whole = parts.reshape(2 * SPAN, COLS)
    high = whole.astype(jnp.bfloat16)
    low = (whole - high.astype(np.float64)).astype(jnp.bfloat16)
    turn = 2.0 * np.pi * (np.arange(RES)[:, None] * bins[None, :]) / (2 * F)
    twiddle = np.stack([np.cos(turn), np.sin(turn)], 1).reshape(2 * RES, SPAN)
    return high, low, twiddle.astype(np.float32)


def dequantize_kernel(codes_ref, exponents_ref, values_ref):
    part = pl.program_id(0)
    _, blocks, chans = exponents_ref.shape
    scale = jnp.exp2(exponents_ref[0].astype(jnp.float32)).T
    scale = scale.astype(jnp.bfloat16).astype(jnp.float32)
    for block in range(blocks):
        wide = jnp.broadcast_to(scale[:, block : block + 1], (chans, LANES))
        at = pl.ds(block * LANES, LANES)
        values_ref[part, :, at] = codes_ref[0, 0, :, at].astype(jnp.float32) * wide


def dequantize(spectra, lanes, seg):
    _, _, chans, nbin = spectra.shape
    return pl.pallas_call(
        dequantize_kernel,
        grid=(2,),
        in_specs=[
            pl.BlockSpec((1, 1, chans, nbin), lambda p: (p, seg, 0, 0)),
            pl.BlockSpec((1, *lanes.shape[1:]), lambda p: (seg, 0, 0)),
        ],
        out_specs=pl.BlockSpec(memory_space=pltpu.VMEM),
        out_shape=jax.ShapeDtypeStruct((2, chans, nbin), jnp.float32),
        compiler_params=pltpu.CompilerParams(vmem_limit_bytes=8 << 20),
        name="dequantize",
    )(spectra, lanes)


def core_of():
    return lax.axis_index("chan") % CORES


def pick_kernel(source_ref, codes_ref, exponents_ref, keep_ref, give_ref, rows_ref, lanes_ref, slab_ref, row_sem, lane_sem):
    segs, blocks, chans = lanes_ref.shape
    local = source_ref[0] - lax.axis_index("chan") * chans
    owned = (local >= 0) & (local < chans)
    row = jnp.clip(local, 0, chans - 1)
    first = pl.multiple_of(row // EIGHT * EIGHT, EIGHT)
    rows_in = pltpu.make_async_copy(codes_ref.at[:, :, pl.ds(first, EIGHT), :], rows_ref, row_sem)
    lanes_in = pltpu.make_async_copy(exponents_ref, lanes_ref, lane_sem)
    rows_in.start()
    lanes_in.start()
    own_lane = lax.broadcasted_iota(jnp.int32, (blocks, chans), 1) == row
    own_row = lax.broadcasted_iota(jnp.int32, (EIGHT, LANES), 0) == row % EIGHT
    lanes_in.wait()
    rows_in.wait()
    groups = SPAN // LANES
    part_groups = groups // CORES
    for g in range(segs):
        exponent = jnp.sum(jnp.where(own_lane, lanes_ref[g].astype(jnp.float32), 0.0), axis=1, keepdims=True)
        scale = jnp.where(owned, jnp.exp2(exponent), 0.0)
        scale = jnp.broadcast_to(scale, (blocks, LANES)).astype(jnp.bfloat16).astype(jnp.float32)
        for part in range(2):
            for block in range(blocks):
                codes = rows_ref[part, g, :, pl.ds(block * LANES, LANES)].astype(jnp.float32)
                code = jnp.sum(jnp.where(own_row, codes, 0.0), axis=0, keepdims=True)
                j, group = divmod(block, groups)
                half, inner = divmod(group, part_groups)
                to = pl.ds((j * part_groups + inner) * LANES, LANES)
                slab_ref[half, pl.ds(part * segs + g, 1), to] = code * scale[block : block + 1]
    keep_ref[...] = slab_ref[core_of()]
    give_ref[...] = slab_ref[CORES - 1 - core_of()]


def pick(source_channels, spectra, lanes):
    _, segs, _, nbin = spectra.shape
    hbm = pl.BlockSpec(memory_space=pltpu.MemorySpace.HBM)
    vmem = pl.BlockSpec(memory_space=pltpu.VMEM)
    half = jax.ShapeDtypeStruct((2 * segs, nbin // CORES), jnp.float32)
    return pl.pallas_call(
        pick_kernel,
        in_specs=[pl.BlockSpec(memory_space=pltpu.SMEM), hbm, hbm],
        out_specs=(vmem, vmem),
        out_shape=(half, half),
        scratch_shapes=[
            pltpu.VMEM((2, segs, EIGHT, nbin), jnp.bfloat16),
            pltpu.VMEM(lanes.shape, jnp.int32),
            pltpu.VMEM((CORES, *half.shape), jnp.float32),
            pltpu.SemaphoreType.DMA(()),
            pltpu.SemaphoreType.DMA(()),
        ],
        compiler_params=pltpu.CompilerParams(vmem_limit_bytes=4 << 20),
        name="pick",
    )(source_channels, spectra, lanes)


def times_root(re, im):
    return (re - im) * ROOT, (re + im) * ROOT


def four(x):
    (ar, ai), (br, bi), (cr, ci), (dr, di) = x
    sr, si, tr, ti = ar + cr, ai + ci, ar - cr, ai - ci
    ur, ui, vr, vi = br + dr, bi + di, br - dr, bi - di
    return [(sr + ur, si + ui), (tr - vi, ti + vr), (sr - ur, si - ui), (tr + vi, ti - vr)]


def lags_kernel(last, first_ref, second_ref, slab_ref, twiddle_ref, high_ref, low_ref, *refs):
    if last:
        sum_ref, out_ref, acc_ref, *parts = refs
        half = CORES - 1 - core_of()
    else:
        acc_ref, *parts = refs
        half = core_of()
    values = (first_ref, second_ref)
    segs = len(values)
    chans = first_ref.shape[1]
    steps = SPAN // LANES // CORES
    tall = RES * ROWS
    slots = (parts[:4], parts[4:])

    def produce(n, slot, begin=0, end=chans):
        def at(j):
            return pl.ds(pl.multiple_of(j * SPAN + (half * steps + n) * LANES, LANES), LANES)

        def slab_at(j):
            return pl.ds(pl.multiple_of((j * steps + n) * LANES, LANES), LANES)

        for r in range(begin, end, ROWS):
            x = []
            for j in range(RES // 2):
                re = im = None
                for g in range(segs):
                    vr = values[g][0, pl.ds(r, ROWS), at(j)]
                    vi = values[g][1, pl.ds(r, ROWS), at(j)]
                    sr = slab_ref[pl.ds(g, 1), slab_at(j)]
                    si = slab_ref[pl.ds(segs + g, 1), slab_at(j)]
                    pr = sr * vr + si * vi
                    pi = sr * vi - si * vr
                    re = pr if re is None else re + pr
                    im = pi if im is None else im + pi
                x.append((re, im))
            even = four(x)
            (br, bi), (dr, di) = x[1], x[3]
            odd = four(
                [
                    x[0],
                    times_root(br, bi),
                    (-x[2][1], x[2][0]),
                    ((-dr - di) * ROOT, (dr - di) * ROOT),
                ]
            )
            for u in range(RES):
                gr, gi = even[u // 2] if u % 2 == 0 else odd[u // 2]
                if u:
                    cos = twiddle_ref[pl.ds(2 * u, 1), at(0)]
                    sin = twiddle_ref[pl.ds(2 * u + 1, 1), at(0)]
                    gr, gi = gr * cos - gi * sin, gr * sin + gi * cos
                rows = pl.ds(r * RES + u * ROWS, ROWS)
                for k, part in enumerate((gr, gi)):
                    top = part.astype(jnp.bfloat16)
                    slots[slot][k][rows, :] = top
                    slots[slot][2 + k][rows, :] = (part - top.astype(jnp.float32)).astype(jnp.bfloat16)

    def contract(n, slot, begin=0, end=chans):
        piece = pl.ds(begin * RES, (end - begin) * RES)
        rows = pl.ds(pl.multiple_of((half * steps + n) * 2 * LANES, 2 * LANES), 2 * LANES)
        table = jnp.concatenate([high_ref[rows, :], high_ref[rows, :], low_ref[rows, :]], axis=0)
        hr, hi, lr, li = (ref[piece, :] for ref in slots[slot])
        both = jnp.concatenate([hr, hi, lr, li, hr, hi], axis=1)
        acc_ref[piece, :] += jnp.dot(both, table, preferred_element_type=jnp.float32)

    acc_ref[...] = sum_ref[...] if last else jnp.zeros_like(acc_ref)
    produce(0, 0)

    def step(n, carry):
        for slot in range(2):

            @pl.when(n % 2 == slot)
            def _():
                for begin in range(0, chans, PIECE):
                    contract(n - 1, 1 - slot, begin, begin + PIECE)
                    produce(n, slot, begin, begin + PIECE)

        return carry

    lax.fori_loop(1, steps, step, 0)
    piece = COLS // RES
    per = LANES // piece
    lane = lax.broadcasted_iota(jnp.int32, (8, LANES), 1)
    for begin in range(0, chans, PIECE):
        contract(steps - 1, (steps - 1) % 2, begin, begin + PIECE)
        if not last:
            continue
        for r in range(begin, begin + PIECE, 8):
            turned = []
            for u in range(RES):
                rows = pl.ds(r // ROWS * tall + u * ROWS + r % ROWS, 8)
                halves = [acc_ref[rows, pl.ds(h * LANES, LANES)] for h in range(2)]
                shift = piece * u
                if shift >= LANES:
                    halves = halves[::-1]
                    shift -= LANES
                if shift:
                    a, b = (pltpu.roll(x, shift, 1) for x in halves)
                    head = lane < shift
                    halves = [jnp.where(head, b, a), jnp.where(head, a, b)]
                turned.append(halves)
            for w in range(RES):
                for h in range(2):
                    picks = [turned[(h * per + s - w) % RES][h] for s in range(per)]
                    left = jnp.where(lane < piece, picks[0], picks[1])
                    right = jnp.where(lane < 3 * piece, picks[2], picks[3])
                    out_ref[w, pl.ds(r, 8), pl.ds(h * LANES, LANES)] = jnp.where(lane < 2 * piece, left, right)


def partial_lags(values, slab, tabs, total=None):
    chans = values[0].shape[1]
    high, low, twiddle = tabs
    vmem = pl.BlockSpec(memory_space=pltpu.VMEM)
    last = total is not None
    sums = (RES * chans, COLS)
    return pl.pallas_call(
        functools.partial(lags_kernel, last),
        in_specs=[vmem] * (7 if last else 6),
        out_specs=vmem,
        out_shape=jax.ShapeDtypeStruct((RES, chans, COLS) if last else sums, jnp.float32),
        scratch_shapes=([pltpu.VMEM(sums, jnp.float32)] if last else [])
        + [pltpu.VMEM((RES * chans, LANES), jnp.bfloat16)] * 8,
        compiler_params=pltpu.CompilerParams(vmem_limit_bytes=12 << 20),
        name="lags",
    )(*values, slab, twiddle, high, low, *([total] if last else []))


def finish_kernel(tiles_ref, out_ref):
    total = tiles_ref[0]
    for peer in range(1, tiles_ref.shape[0]):
        total = total + tiles_ref[peer]
    piece = COLS // RES
    place = lax.broadcasted_iota(jnp.int32, (COLS, COLS), 0)
    lag = lax.broadcasted_iota(jnp.int32, (COLS, COLS), 1)
    residue = ((place >> 5) - lax.axis_index("win") + RES) & (RES - 1)
    order = jnp.where(lag == (place & (piece - 1)) * RES + residue, 1.0, 0.0).astype(jnp.bfloat16)
    first = total.astype(jnp.bfloat16)
    rest = total - first.astype(jnp.float32)
    second = rest.astype(jnp.bfloat16)
    third = (rest - second.astype(jnp.float32)).astype(jnp.bfloat16)
    dot = lambda a: jnp.dot(a, order, preferred_element_type=jnp.float32)
    out_ref[...] = (dot(third) + dot(second)) + dot(first)


def finish(tiles):
    return pl.pallas_call(
        finish_kernel,
        in_specs=[pl.BlockSpec(memory_space=pltpu.VMEM)],
        out_specs=pl.BlockSpec(memory_space=pltpu.VMEM),
        out_shape=jax.ShapeDtypeStruct(tiles.shape[1:], jnp.float32),
        compiler_params=pltpu.CompilerParams(vmem_limit_bytes=8 << 20),
        name="finish",
    )(tiles)


def swap(array, bit):
    peers = lax.axis_size("chan")
    return lax.ppermute(array, "chan", [(peer, peer ^ bit) for peer in range(peers)])


def body(spectra, exponents, source_channels):
    segs = spectra.shape[1] * lax.axis_size("win")
    stay = lambda array: pltpu.with_memory_space_constraint(array, pltpu.MemorySpace.HBM)
    spectra = stay(spectra)
    lanes = stay(jnp.transpose(exponents, (0, 2, 1)))
    tabs = tables(1.0 / math.sqrt(4.0 * F * segs))
    keep, give = pick(source_channels, spectra, lanes)
    own = keep + swap(give, 1)
    own, first = lax.optimization_barrier((own + swap(own, 16), dequantize(spectra, lanes, 0)))
    own = own + swap(own, 2)
    own, second = lax.optimization_barrier((own + swap(own, 4), dequantize(spectra, lanes, 1)))
    own = own + swap(own, 12)
    other = swap(own, 1)
    total = partial_lags((first, second), own, tabs)
    partial = partial_lags((first, second), other, tabs, total)
    return finish(lax.all_to_all(partial, "win", 0, 0, tiled=True))[None]


def solution(mesh):
    return jax.shard_map(
        body,
        mesh=mesh,
        in_specs=(P(None, "win", "chan", None), P("win", "chan", None), P()),
        out_specs=P(None, "chan", "win"),
        check_vma=False,
    )
```

```python
import math

import jax
import jax.numpy as jnp
import numpy as np
from jax import lax
from jax.experimental import pallas as pl
from jax.experimental.pallas import tpu as pltpu
from jax.sharding import PartitionSpec as P

F = 4096
L = 2048
RES = 8
SPAN = 2 * F // RES
COLS = L // RES
LANES = 128
ROWS = 16
PIECE = 32
EIGHT = 8
ROOT = math.sqrt(0.5)


def tables(norm):
    bins = np.arange(SPAN)
    lag = np.arange(COLS) - COLS // 2
    angle = 2.0 * np.pi * ((bins[:, None] * lag[None, :]) % SPAN) / SPAN
    parts = np.stack([np.cos(angle), -np.sin(angle)], 0) * norm
    parts = parts.reshape(2, SPAN // LANES, LANES, COLS).transpose(1, 0, 2, 3)
    whole = parts.reshape(2 * SPAN, COLS)
    high = whole.astype(jnp.bfloat16)
    low = (whole - high.astype(np.float64)).astype(jnp.bfloat16)
    turn = 2.0 * np.pi * (np.arange(RES)[:, None] * bins[None, :]) / (2 * F)
    twiddle = np.stack([np.cos(turn), np.sin(turn)], 1).reshape(2 * RES, SPAN)
    return high, low, twiddle.astype(np.float32)


def dequantize_kernel(codes_ref, exponents_ref, values_ref):
    part = pl.program_id(0)
    _, blocks, chans = exponents_ref.shape
    scale = jnp.exp2(exponents_ref[0].astype(jnp.float32)).T
    scale = scale.astype(jnp.bfloat16).astype(jnp.float32)
    for block in range(blocks):
        wide = jnp.broadcast_to(scale[:, block : block + 1], (chans, LANES))
        at = pl.ds(block * LANES, LANES)
        values_ref[part, :, at] = codes_ref[0, 0, :, at].astype(jnp.float32) * wide


def dequantize(spectra, lanes, seg):
    _, _, chans, nbin = spectra.shape
    return pl.pallas_call(
        dequantize_kernel,
        grid=(2,),
        in_specs=[
            pl.BlockSpec((1, 1, chans, nbin), lambda p: (p, seg, 0, 0)),
            pl.BlockSpec((1, *lanes.shape[1:]), lambda p: (seg, 0, 0)),
        ],
        out_specs=pl.BlockSpec(memory_space=pltpu.VMEM),
        out_shape=jax.ShapeDtypeStruct((2, chans, nbin), jnp.float32),
        compiler_params=pltpu.CompilerParams(vmem_limit_bytes=8 << 20),
        name="dequantize",
    )(spectra, lanes)


def pick_kernel(source_ref, codes_ref, exponents_ref, slab_ref, rows_ref, lanes_ref, row_sem, lane_sem):
    segs, blocks, chans = lanes_ref.shape
    local = source_ref[0] - lax.axis_index("chan") * chans
    owned = (local >= 0) & (local < chans)
    row = jnp.clip(local, 0, chans - 1)
    first = pl.multiple_of(row // EIGHT * EIGHT, EIGHT)
    rows_in = pltpu.make_async_copy(codes_ref.at[:, :, pl.ds(first, EIGHT), :], rows_ref, row_sem)
    lanes_in = pltpu.make_async_copy(exponents_ref, lanes_ref, lane_sem)
    rows_in.start()
    lanes_in.start()
    own_lane = lax.broadcasted_iota(jnp.int32, (blocks, chans), 1) == row
    own_row = lax.broadcasted_iota(jnp.int32, (EIGHT, LANES), 0) == row % EIGHT
    lanes_in.wait()
    rows_in.wait()
    for g in range(segs):
        exponent = jnp.sum(jnp.where(own_lane, lanes_ref[g].astype(jnp.float32), 0.0), axis=1, keepdims=True)
        scale = jnp.where(owned, jnp.exp2(exponent), 0.0)
        scale = jnp.broadcast_to(scale, (blocks, LANES)).astype(jnp.bfloat16).astype(jnp.float32)
        for part in range(2):
            for block in range(blocks):
                at = pl.ds(block * LANES, LANES)
                codes = rows_ref[part, g, :, at].astype(jnp.float32)
                code = jnp.sum(jnp.where(own_row, codes, 0.0), axis=0, keepdims=True)
                slab_ref[pl.ds(part * segs + g, 1), at] = code * scale[block : block + 1]


def pick(source_channels, spectra, lanes):
    _, segs, _, nbin = spectra.shape
    hbm = pl.BlockSpec(memory_space=pltpu.MemorySpace.HBM)
    return pl.pallas_call(
        pick_kernel,
        in_specs=[pl.BlockSpec(memory_space=pltpu.SMEM), hbm, hbm],
        out_specs=pl.BlockSpec(memory_space=pltpu.VMEM),
        out_shape=jax.ShapeDtypeStruct((2 * segs, nbin), jnp.float32),
        scratch_shapes=[
            pltpu.VMEM((2, segs, EIGHT, nbin), jnp.bfloat16),
            pltpu.VMEM(lanes.shape, jnp.int32),
            pltpu.SemaphoreType.DMA(()),
            pltpu.SemaphoreType.DMA(()),
        ],
        compiler_params=pltpu.CompilerParams(vmem_limit_bytes=4 << 20),
        name="pick",
    )(source_channels, spectra, lanes)


def times_root(re, im):
    return (re - im) * ROOT, (re + im) * ROOT


def four(x):
    (ar, ai), (br, bi), (cr, ci), (dr, di) = x
    sr, si, tr, ti = ar + cr, ai + ci, ar - cr, ai - ci
    ur, ui, vr, vi = br + dr, bi + di, br - dr, bi - di
    return [(sr + ur, si + ui), (tr - vi, ti + vr), (sr - ur, si - ui), (tr + vi, ti - vr)]


def lags_kernel(first_ref, second_ref, slab_ref, twiddle_ref, high_ref, low_ref, out_ref, acc_ref, *parts):
    chans = out_ref.shape[1]
    values = (first_ref, second_ref)
    segs = len(values)
    steps = SPAN // LANES
    tall = RES * ROWS
    slots = (parts[:4], parts[4:])

    def produce(n, slot, begin=0, end=chans):
        def at(j):
            return pl.ds(pl.multiple_of(j * SPAN + n * LANES, LANES), LANES)

        for r in range(begin, end, ROWS):
            x = []
            for j in range(RES // 2):
                re = im = None
                for g in range(segs):
                    vr = values[g][0, pl.ds(r, ROWS), at(j)]
                    vi = values[g][1, pl.ds(r, ROWS), at(j)]
                    sr = slab_ref[pl.ds(g, 1), at(j)]
                    si = slab_ref[pl.ds(segs + g, 1), at(j)]
                    pr = sr * vr + si * vi
                    pi = sr * vi - si * vr
                    re = pr if re is None else re + pr
                    im = pi if im is None else im + pi
                x.append((re, im))
            even = four(x)
            (br, bi), (dr, di) = x[1], x[3]
            odd = four(
                [
                    x[0],
                    times_root(br, bi),
                    (-x[2][1], x[2][0]),
                    ((-dr - di) * ROOT, (dr - di) * ROOT),
                ]
            )
            for u in range(RES):
                gr, gi = even[u // 2] if u % 2 == 0 else odd[u // 2]
                if u:
                    cos = twiddle_ref[pl.ds(2 * u, 1), at(0)]
                    sin = twiddle_ref[pl.ds(2 * u + 1, 1), at(0)]
                    gr, gi = gr * cos - gi * sin, gr * sin + gi * cos
                rows = pl.ds(r * RES + u * ROWS, ROWS)
                for k, part in enumerate((gr, gi)):
                    top = part.astype(jnp.bfloat16)
                    slots[slot][k][rows, :] = top
                    slots[slot][2 + k][rows, :] = (part - top.astype(jnp.float32)).astype(jnp.bfloat16)

    def contract(n, slot, begin=0, end=chans):
        piece = pl.ds(begin * RES, (end - begin) * RES)
        rows = pl.ds(pl.multiple_of(n * 2 * LANES, 2 * LANES), 2 * LANES)
        table = jnp.concatenate([high_ref[rows, :], high_ref[rows, :], low_ref[rows, :]], axis=0)
        hr, hi, lr, li = (ref[piece, :] for ref in slots[slot])
        both = jnp.concatenate([hr, hi, lr, li, hr, hi], axis=1)
        acc_ref[piece, :] += jnp.dot(both, table, preferred_element_type=jnp.float32)

    acc_ref[...] = jnp.zeros_like(acc_ref)
    produce(0, 0)

    def step(n, carry):
        for slot in range(2):

            @pl.when(n % 2 == slot)
            def _():
                for begin in range(0, chans, PIECE):
                    contract(n - 1, 1 - slot, begin, begin + PIECE)
                    produce(n, slot, begin, begin + PIECE)

        return carry

    lax.fori_loop(1, steps, step, 0)
    piece = COLS // RES
    per = LANES // piece
    lane = lax.broadcasted_iota(jnp.int32, (8, LANES), 1)
    for begin in range(0, chans, PIECE):
        contract(steps - 1, (steps - 1) % 2, begin, begin + PIECE)
        for r in range(begin, begin + PIECE, 8):
            turned = []
            for u in range(RES):
                rows = pl.ds(r // ROWS * tall + u * ROWS + r % ROWS, 8)
                halves = [acc_ref[rows, pl.ds(h * LANES, LANES)] for h in range(2)]
                shift = piece * u
                if shift >= LANES:
                    halves = halves[::-1]
                    shift -= LANES
                if shift:
                    a, b = (pltpu.roll(x, shift, 1) for x in halves)
                    head = lane < shift
                    halves = [jnp.where(head, b, a), jnp.where(head, a, b)]
                turned.append(halves)
            for w in range(RES):
                for h in range(2):
                    picks = [turned[(h * per + s - w) % RES][h] for s in range(per)]
                    left = jnp.where(lane < piece, picks[0], picks[1])
                    right = jnp.where(lane < 3 * piece, picks[2], picks[3])
                    out_ref[w, pl.ds(r, 8), pl.ds(h * LANES, LANES)] = jnp.where(lane < 2 * piece, left, right)


def partial_lags(values, slab, tabs):
    chans = values[0].shape[1]
    high, low, twiddle = tabs
    vmem = pl.BlockSpec(memory_space=pltpu.VMEM)
    return pl.pallas_call(
        lags_kernel,
        in_specs=[vmem] * 6,
        out_specs=vmem,
        out_shape=jax.ShapeDtypeStruct((RES, chans, COLS), jnp.float32),
        scratch_shapes=[pltpu.VMEM((RES * chans, COLS), jnp.float32)]
        + [pltpu.VMEM((RES * chans, LANES), jnp.bfloat16)] * 8,
        compiler_params=pltpu.CompilerParams(vmem_limit_bytes=16 << 20),
        name="lags",
    )(*values, slab, twiddle, high, low)


def finish_kernel(tiles_ref, out_ref):
    total = tiles_ref[0]
    for peer in range(1, tiles_ref.shape[0]):
        total = total + tiles_ref[peer]
    piece = COLS // RES
    place = lax.broadcasted_iota(jnp.int32, (COLS, COLS), 0)
    lag = lax.broadcasted_iota(jnp.int32, (COLS, COLS), 1)
    residue = ((place >> 5) - lax.axis_index("win") + RES) & (RES - 1)
    order = jnp.where(lag == (place & (piece - 1)) * RES + residue, 1.0, 0.0).astype(jnp.bfloat16)
    first = total.astype(jnp.bfloat16)
    rest = total - first.astype(jnp.float32)
    second = rest.astype(jnp.bfloat16)
    third = (rest - second.astype(jnp.float32)).astype(jnp.bfloat16)
    dot = lambda a: jnp.dot(a, order, preferred_element_type=jnp.float32)
    out_ref[...] = (dot(third) + dot(second)) + dot(first)


def finish(tiles):
    return pl.pallas_call(
        finish_kernel,
        in_specs=[pl.BlockSpec(memory_space=pltpu.VMEM)],
        out_specs=pl.BlockSpec(memory_space=pltpu.VMEM),
        out_shape=jax.ShapeDtypeStruct(tiles.shape[1:], jnp.float32),
        compiler_params=pltpu.CompilerParams(vmem_limit_bytes=8 << 20),
        name="finish",
    )(tiles)


def exchange(slab, *bits):
    peers = lax.axis_size("chan")
    moved = [lax.ppermute(slab, "chan", [(peer, peer ^ bit) for peer in range(peers)]) for bit in bits]
    return sum(moved, slab)


def body(spectra, exponents, source_channels):
    segs = spectra.shape[1] * lax.axis_size("win")
    stay = lambda array: pltpu.with_memory_space_constraint(array, pltpu.MemorySpace.HBM)
    spectra = stay(spectra)
    lanes = stay(jnp.transpose(exponents, (0, 2, 1)))
    slab = pick(source_channels, spectra, lanes)
    slab = exchange(slab, 1)
    slab, first = lax.optimization_barrier((exchange(slab, 16), dequantize(spectra, lanes, 0)))
    slab, second = lax.optimization_barrier((exchange(slab, 4, 2, 6), dequantize(spectra, lanes, 1)))
    slab = exchange(slab, 12)
    tabs = tables(1.0 / math.sqrt(4.0 * F * segs))
    partial = partial_lags((first, second), slab, tabs)
    return finish(lax.all_to_all(partial, "win", 0, 0, tiled=True))[None]


def solution(mesh):
    return jax.shard_map(
        body,
        mesh=mesh,
        in_specs=(P(None, "win", "chan", None), P("win", "chan", None), P()),
        out_specs=P(None, "chan", "win"),
        check_vma=False,
    )
```

```python
import math

import jax
import jax.numpy as jnp
import numpy as np
from jax import lax
from jax.experimental import pallas as pl
from jax.experimental.pallas import tpu as pltpu
from jax.sharding import PartitionSpec as P

F = 4096
L = 2048
RES = 8
SPAN = 2 * F // RES
COLS = L // RES
LANES = 128
ROWS = 16
PIECE = 32
EIGHT = 8
ROOT = math.sqrt(0.5)


def tables(norm):
    bins = np.arange(SPAN)
    lag = np.arange(COLS) - COLS // 2
    angle = 2.0 * np.pi * ((bins[:, None] * lag[None, :]) % SPAN) / SPAN
    parts = np.stack([np.cos(angle), -np.sin(angle)], 0) * norm
    parts = parts.reshape(2, SPAN // LANES, LANES, COLS).transpose(1, 0, 2, 3)
    whole = parts.reshape(2 * SPAN, COLS)
    high = whole.astype(jnp.bfloat16)
    low = (whole - high.astype(np.float64)).astype(jnp.bfloat16)
    turn = 2.0 * np.pi * (np.arange(RES)[:, None] * bins[None, :]) / (2 * F)
    twiddle = np.stack([np.cos(turn), np.sin(turn)], 1).reshape(2 * RES, SPAN)
    return high, low, twiddle.astype(np.float32)


def dequantize_kernel(codes_ref, exponents_ref, values_ref):
    part = pl.program_id(0)
    _, blocks, chans = exponents_ref.shape
    scale = jnp.exp2(exponents_ref[0].astype(jnp.float32)).T
    scale = scale.astype(jnp.bfloat16).astype(jnp.float32)
    for block in range(blocks):
        wide = jnp.broadcast_to(scale[:, block : block + 1], (chans, LANES))
        at = pl.ds(block * LANES, LANES)
        values_ref[part, :, at] = codes_ref[0, 0, :, at].astype(jnp.float32) * wide


def dequantize(spectra, lanes, seg):
    _, _, chans, nbin = spectra.shape
    return pl.pallas_call(
        dequantize_kernel,
        grid=(2,),
        in_specs=[
            pl.BlockSpec((1, 1, chans, nbin), lambda p: (p, seg, 0, 0)),
            pl.BlockSpec((1, *lanes.shape[1:]), lambda p: (seg, 0, 0)),
        ],
        out_specs=pl.BlockSpec(memory_space=pltpu.VMEM),
        out_shape=jax.ShapeDtypeStruct((2, chans, nbin), jnp.float32),
        compiler_params=pltpu.CompilerParams(vmem_limit_bytes=8 << 20),
        name="dequantize",
    )(spectra, lanes)


def pick_kernel(source_ref, codes_ref, exponents_ref, slab_ref, rows_ref, lanes_ref, row_sem, lane_sem):
    segs, blocks, chans = lanes_ref.shape
    local = source_ref[0] - lax.axis_index("chan") * chans
    owned = (local >= 0) & (local < chans)
    row = jnp.clip(local, 0, chans - 1)
    first = pl.multiple_of(row // EIGHT * EIGHT, EIGHT)
    slab_ref[...] = jnp.zeros_like(slab_ref)

    @pl.when(owned)
    def _():
        rows_in = pltpu.make_async_copy(codes_ref.at[:, :, pl.ds(first, EIGHT), :], rows_ref, row_sem)
        lanes_in = pltpu.make_async_copy(exponents_ref, lanes_ref, lane_sem)
        rows_in.start()
        lanes_in.start()
        own_lane = lax.broadcasted_iota(jnp.int32, (blocks, chans), 1) == row
        own_row = lax.broadcasted_iota(jnp.int32, (EIGHT, LANES), 0) == row % EIGHT
        lanes_in.wait()
        rows_in.wait()
        for g in range(segs):
            exponent = jnp.sum(jnp.where(own_lane, lanes_ref[g].astype(jnp.float32), 0.0), axis=1, keepdims=True)
            scale = jnp.exp2(exponent)
            scale = jnp.broadcast_to(scale, (blocks, LANES)).astype(jnp.bfloat16).astype(jnp.float32)
            for part in range(2):
                for block in range(blocks):
                    at = pl.ds(block * LANES, LANES)
                    codes = rows_ref[part, g, :, at].astype(jnp.float32)
                    code = jnp.sum(jnp.where(own_row, codes, 0.0), axis=0, keepdims=True)
                    slab_ref[pl.ds(part * segs + g, 1), at] = code * scale[block : block + 1]


def pick(source_channels, spectra, lanes):
    _, segs, _, nbin = spectra.shape
    hbm = pl.BlockSpec(memory_space=pltpu.MemorySpace.HBM)
    return pl.pallas_call(
        pick_kernel,
        in_specs=[pl.BlockSpec(memory_space=pltpu.SMEM), hbm, hbm],
        out_specs=pl.BlockSpec(memory_space=pltpu.VMEM),
        out_shape=jax.ShapeDtypeStruct((2 * segs, nbin), jnp.float32),
        scratch_shapes=[
            pltpu.VMEM((2, segs, EIGHT, nbin), jnp.bfloat16),
            pltpu.VMEM(lanes.shape, jnp.int32),
            pltpu.SemaphoreType.DMA(()),
            pltpu.SemaphoreType.DMA(()),
        ],
        compiler_params=pltpu.CompilerParams(vmem_limit_bytes=4 << 20),
        name="pick",
    )(source_channels, spectra, lanes)


def times_root(re, im):
    return (re - im) * ROOT, (re + im) * ROOT


def four(x):
    (ar, ai), (br, bi), (cr, ci), (dr, di) = x
    sr, si, tr, ti = ar + cr, ai + ci, ar - cr, ai - ci
    ur, ui, vr, vi = br + dr, bi + di, br - dr, bi - di
    return [(sr + ur, si + ui), (tr - vi, ti + vr), (sr - ur, si - ui), (tr + vi, ti - vr)]


def lags_kernel(first_ref, second_ref, slab_ref, twiddle_ref, high_ref, low_ref, out_ref, acc_ref, *parts):
    chans = out_ref.shape[1]
    values = (first_ref, second_ref)
    segs = len(values)
    steps = SPAN // LANES
    tall = RES * ROWS
    slots = (parts[:4], parts[4:])

    def produce(n, slot, begin=0, end=chans):
        def at(j):
            return pl.ds(pl.multiple_of(j * SPAN + n * LANES, LANES), LANES)

        for r in range(begin, end, ROWS):
            x = []
            for j in range(RES // 2):
                re = im = None
                for g in range(segs):
                    vr = values[g][0, pl.ds(r, ROWS), at(j)]
                    vi = values[g][1, pl.ds(r, ROWS), at(j)]
                    sr = slab_ref[pl.ds(g, 1), at(j)]
                    si = slab_ref[pl.ds(segs + g, 1), at(j)]
                    pr = sr * vr + si * vi
                    pi = sr * vi - si * vr
                    re = pr if re is None else re + pr
                    im = pi if im is None else im + pi
                x.append((re, im))
            even = four(x)
            (br, bi), (dr, di) = x[1], x[3]
            odd = four(
                [
                    x[0],
                    times_root(br, bi),
                    (-x[2][1], x[2][0]),
                    ((-dr - di) * ROOT, (dr - di) * ROOT),
                ]
            )
            for u in range(RES):
                gr, gi = even[u // 2] if u % 2 == 0 else odd[u // 2]
                if u:
                    cos = twiddle_ref[pl.ds(2 * u, 1), at(0)]
                    sin = twiddle_ref[pl.ds(2 * u + 1, 1), at(0)]
                    gr, gi = gr * cos - gi * sin, gr * sin + gi * cos
                rows = pl.ds(r * RES + u * ROWS, ROWS)
                for k, part in enumerate((gr, gi)):
                    top = part.astype(jnp.bfloat16)
                    slots[slot][k][rows, :] = top
                    slots[slot][2 + k][rows, :] = (part - top.astype(jnp.float32)).astype(jnp.bfloat16)

    def contract(n, slot, begin=0, end=chans):
        piece = pl.ds(begin * RES, (end - begin) * RES)
        rows = pl.ds(pl.multiple_of(n * 2 * LANES, 2 * LANES), 2 * LANES)
        table = jnp.concatenate([high_ref[rows, :], high_ref[rows, :], low_ref[rows, :]], axis=0)
        hr, hi, lr, li = (ref[piece, :] for ref in slots[slot])
        both = jnp.concatenate([hr, hi, lr, li, hr, hi], axis=1)
        acc_ref[piece, :] += jnp.dot(both, table, preferred_element_type=jnp.float32)

    acc_ref[...] = jnp.zeros_like(acc_ref)
    produce(0, 0)

    def step(n, carry):
        for slot in range(2):

            @pl.when(n % 2 == slot)
            def _():
                for begin in range(0, chans, PIECE):
                    contract(n - 1, 1 - slot, begin, begin + PIECE)
                    produce(n, slot, begin, begin + PIECE)

        return carry

    lax.fori_loop(1, steps, step, 0)
    piece = COLS // RES
    per = LANES // piece
    lane = lax.broadcasted_iota(jnp.int32, (8, LANES), 1)
    for begin in range(0, chans, PIECE):
        contract(steps - 1, (steps - 1) % 2, begin, begin + PIECE)
        for r in range(begin, begin + PIECE, 8):
            turned = []
            for u in range(RES):
                rows = pl.ds(r // ROWS * tall + u * ROWS + r % ROWS, 8)
                halves = [acc_ref[rows, pl.ds(h * LANES, LANES)] for h in range(2)]
                shift = piece * u
                if shift >= LANES:
                    halves = halves[::-1]
                    shift -= LANES
                if shift:
                    a, b = (pltpu.roll(x, shift, 1) for x in halves)
                    head = lane < shift
                    halves = [jnp.where(head, b, a), jnp.where(head, a, b)]
                turned.append(halves)
            for w in range(RES):
                for h in range(2):
                    picks = [turned[(h * per + s - w) % RES][h] for s in range(per)]
                    left = jnp.where(lane < piece, picks[0], picks[1])
                    right = jnp.where(lane < 3 * piece, picks[2], picks[3])
                    out_ref[w, pl.ds(r, 8), pl.ds(h * LANES, LANES)] = jnp.where(lane < 2 * piece, left, right)


def partial_lags(values, slab, tabs):
    chans = values[0].shape[1]
    high, low, twiddle = tabs
    vmem = pl.BlockSpec(memory_space=pltpu.VMEM)
    return pl.pallas_call(
        lags_kernel,
        in_specs=[vmem] * 6,
        out_specs=vmem,
        out_shape=jax.ShapeDtypeStruct((RES, chans, COLS), jnp.float32),
        scratch_shapes=[pltpu.VMEM((RES * chans, COLS), jnp.float32)]
        + [pltpu.VMEM((RES * chans, LANES), jnp.bfloat16)] * 8,
        compiler_params=pltpu.CompilerParams(vmem_limit_bytes=16 << 20),
        name="lags",
    )(*values, slab, twiddle, high, low)


def finish_kernel(tiles_ref, out_ref):
    total = tiles_ref[0]
    for peer in range(1, tiles_ref.shape[0]):
        total = total + tiles_ref[peer]
    piece = COLS // RES
    place = lax.broadcasted_iota(jnp.int32, (COLS, COLS), 0)
    lag = lax.broadcasted_iota(jnp.int32, (COLS, COLS), 1)
    residue = ((place >> 5) - lax.axis_index("win") + RES) & (RES - 1)
    order = jnp.where(lag == (place & (piece - 1)) * RES + residue, 1.0, 0.0).astype(jnp.bfloat16)
    first = total.astype(jnp.bfloat16)
    rest = total - first.astype(jnp.float32)
    second = rest.astype(jnp.bfloat16)
    third = (rest - second.astype(jnp.float32)).astype(jnp.bfloat16)
    dot = lambda a: jnp.dot(a, order, preferred_element_type=jnp.float32)
    out_ref[...] = (dot(third) + dot(second)) + dot(first)


def finish(tiles):
    return pl.pallas_call(
        finish_kernel,
        in_specs=[pl.BlockSpec(memory_space=pltpu.VMEM)],
        out_specs=pl.BlockSpec(memory_space=pltpu.VMEM),
        out_shape=jax.ShapeDtypeStruct(tiles.shape[1:], jnp.float32),
        compiler_params=pltpu.CompilerParams(vmem_limit_bytes=8 << 20),
        name="finish",
    )(tiles)


def exchange(slab, *bits):
    peers = lax.axis_size("chan")
    moved = [lax.ppermute(slab, "chan", [(peer, peer ^ bit) for peer in range(peers)]) for bit in bits]
    return sum(moved, slab)


def body(spectra, exponents, source_channels):
    segs = spectra.shape[1] * lax.axis_size("win")
    stay = lambda array: pltpu.with_memory_space_constraint(array, pltpu.MemorySpace.HBM)
    spectra = stay(spectra)
    lanes = stay(jnp.transpose(exponents, (0, 2, 1)))
    slab = pick(source_channels, spectra, lanes)
    slab = exchange(slab, 1)
    slab, first = lax.optimization_barrier((exchange(slab, 16), dequantize(spectra, lanes, 0)))
    slab, second = lax.optimization_barrier((exchange(slab, 4, 2, 6), dequantize(spectra, lanes, 1)))
    slab = exchange(slab, 12)
    tabs = tables(1.0 / math.sqrt(4.0 * F * segs))
    partial = partial_lags((first, second), slab, tabs)
    return finish(lax.all_to_all(partial, "win", 0, 0, tiled=True))[None]


def solution(mesh):
    return jax.shard_map(
        body,
        mesh=mesh,
        in_specs=(P(None, "win", "chan", None), P("win", "chan", None), P()),
        out_specs=P(None, "chan", "win"),
        check_vma=False,
    )
```
